32 devices in a mesh: seq: 4 (over y, core), ctx: 8 (over z, x).
Axes of the slice: x: 2, y: 2, z: 4, core: 2. Of those that a mesh axis runs over, the one named last changes fastest.
Arguments:
- tokens: bfloat16 [8, 2048, 2048], P('seq', 'ctx'), may hold values from -6 to 6
- out_grad: bfloat16 [8, 2048, 2048], P('seq', 'ctx'), may hold values from -6 to 6
- doc_ids: int32 [8, 2048], P('seq', 'ctx'), may hold values from 0 to 5, never falling along the last dimension, each value on 1 to 1024 neighbouring positions
- corpus: int32 [8], P('seq'), may hold values from 0 to 3
- corpus_weight: float32 [4], replicated, may hold values from 0.3 to 3
- attn_gain: bfloat16 [2048], P(('seq', 'ctx')), may hold values from 0.5 to 1.5
- w_query: bfloat16 [2048, 1280], P(('seq', 'ctx')), may hold values from -0.125 to 0.125
- w_key: bfloat16 [2048, 320], P(('seq', 'ctx')), may hold values from -0.125 to 0.125
- w_value: bfloat16 [2048, 320], P(('seq', 'ctx')), may hold values from -0.125 to 0.125
- query_gain: bfloat16 [64], replicated, may hold values from 0.099609375 to 1.8984375
- key_gain: bfloat16 [64], replicated, may hold values from 0.099609375 to 1.8984375
- w_out: bfloat16 [1280, 2048], P(('seq', 'ctx')), may hold values from -1.25 to 1.25
- ffn_gain: bfloat16 [2048], P(('seq', 'ctx')), may hold values from 0.5 to 1.5
- w_gate: bfloat16 [2048, 3584], P(('seq', 'ctx')), may hold values from -0.125 to 0.125
- w_up: bfloat16 [2048, 3584], P(('seq', 'ctx')), may hold values from -0.125 to 0.125
- w_down: bfloat16 [3584, 2048], P(('seq', 'ctx')), may hold values from -0.09375 to 0.09375
Outputs:
- layer_out: bfloat16 [8, 2048, 2048], P('seq', 'ctx')
- tokens_grad: bfloat16 [8, 2048, 2048], P('seq', 'ctx')
- attn_gain_grad: float32 [2048], P(('seq', 'ctx'))
- w_query_grad: float32 [2048, 1280], P(('seq', 'ctx'))
- w_key_grad: float32 [2048, 320], P(('seq', 'ctx'))
- w_value_grad: float32 [2048, 320], P(('seq', 'ctx'))
- query_gain_grad: float32 [64], replicated
- key_gain_grad: float32 [64], replicated
- w_out_grad: float32 [1280, 2048], P(('seq', 'ctx'))
- ffn_gain_grad: float32 [2048], P(('seq', 'ctx'))
- w_gate_grad: float32 [2048, 3584], P(('seq', 'ctx'))
- w_up_grad: float32 [2048, 3584], P(('seq', 'ctx'))
- w_down_grad: float32 [3584, 2048], P(('seq', 'ctx'))
The draws below stay inside these ranges and needn't reach their ends.
Inputs may be any that keep to these rules, and one draw needn't show every extreme that they name: `doc_ids`: within a sequence ids never fall, and each document spans at most 1024 positions.
All inputs are finite; a program needn't handle non-finite values.
Results may differ from the reference program's by a relative error of at most 0.017.
Values may be sent and summed in bfloat16 or wider, within the bound.
No kernel may reach another device: no remote copies, remote signals or barrier semaphores. Data moves between devices by JAX's collectives and lax.ppermute only.
A program may use at most 512 MiB of HBM per device.

```python
import math
import jax
import jax.numpy as jnp
import numpy as np
from jax import lax

D = 2048
FF = 3584
HEADS = 20
KV_HEADS = 5
HEAD_DIM = 64
SEQ_LEN = 2048
QROWS = 512
TAGS = 4
DOCS = 6
DOC_MOST = 1024
SEQS = 8
Q_WIDTH = 1280
KV_WIDTH = 320


def set_ends(array, stream_key, least, largest):
    extent = array.shape
    spot = [jax.random.randint(jax.random.fold_in(stream_key, axis), (), 0, extent[axis]) for axis in range(len(extent))]
    array = array.at[tuple(spot)].set(least)
    longest = extent.index(max(extent))
    spot[longest] = (spot[longest] + 1) % extent[longest]
    return array.at[tuple(spot)].set(largest)


def block_levels(rng, shape, cuts, low, high):
    loudness, own = 1.0, jax.random.fold_in(rng, 6)
    for axis_at, blocks in cuts:
        draws = jnp.exp(jax.random.uniform(jax.random.fold_in(own, axis_at), (blocks,), jnp.float32, low / len(cuts), high / len(cuts)))
        loudness = loudness * jnp.repeat(draws, shape[axis_at] // blocks).reshape([-1 if axis == axis_at else 1 for axis in range(len(shape))])
    return loudness


def profile(number_of, total, bound, lean):
    weights = [(1 << 20) // math.isqrt(rank ** lean) + 1 for rank in range(2, number_of + 1)]
    spare, given = total - bound - (number_of - 1), [1] * (number_of - 1)
    while spare > 0:
        candidates = [i for i in range(number_of - 1) if given[i] < bound]
        whole, remaining = sum([weights[i] for i in candidates]), spare
        for i in candidates:
            addition = min(bound - given[i], max(1, remaining * weights[i] // whole), spare)
            given[i] = given[i] + addition
            spare = spare - addition
    return np.array([bound] + given)


def uneven(stream_key, count, total, limit, skew):
    if count == 2:
        one = jax.random.randint(stream_key, (), max(1, total - limit), min(limit, total - 1) + 1)
        return jnp.stack([one, total - one])
    lengths = jnp.asarray(profile(count, total, limit, skew), jnp.int32)
    couples = (count - 1) // 2
    donor, taker = lengths[1:1 + 2 * couples:2], lengths[2:2 + 2 * couples:2]
    room = jnp.minimum(donor - 1, limit - taker)
    moved = jax.random.randint(jax.random.fold_in(stream_key, 1), (couples,), 0, 1 << 20) % (room + 1)
    lengths = lengths.at[1:1 + 2 * couples:2].set(donor - moved).at[2:2 + 2 * couples:2].set(taker + moved)
    return lengths[jax.random.permutation(jax.random.fold_in(stream_key, 2), count)]


def noise(rng, dims, spread, limit, cuts=(), kind=jnp.bfloat16):
    gain = block_levels(rng, dims, cuts, -0.22, 0.18) if cuts else 1.0
    array = jax.random.normal(rng, dims, jnp.float32) * spread * gain
    return jnp.minimum(jnp.maximum(array, -limit), limit).astype(kind)


def setup_inputs(seed: int = 0) -> dict:
    key_list = jax.random.split(jax.random.key(seed), 17)
    return {
        "tokens": noise(key_list[0], (SEQS, SEQ_LEN, D), 1.0, 6.0, ((0, 4), (1, 8))),
        "out_grad": noise(key_list[1], (SEQS, SEQ_LEN, D), 1.0, 6.0, ((0, 4), (1, 8))),
        "doc_ids": jax.vmap(lambda own: jnp.searchsorted(jnp.cumsum(uneven(own, DOCS, SEQ_LEN, DOC_MOST, 2)), jnp.arange(SEQ_LEN), side="right"))(jax.random.split(key_list[2], SEQS)).reshape((SEQS, SEQ_LEN)).astype(jnp.int32),
        "corpus": set_ends(jax.random.randint(key_list[3], (SEQS,), 0, TAGS), jax.random.fold_in(key_list[3], 1), 0, TAGS - 1).astype(jnp.int32),
        "corpus_weight": jnp.clip(jnp.exp(jax.random.uniform(key_list[4], (TAGS,), jnp.float32, math.log(0.3), math.log(3.0))), 0.3, 3.0),
        "attn_gain": jnp.clip(1.0 + 0.1 * jax.random.normal(key_list[5], (D,), jnp.float32), 0.5, 1.5).astype(jnp.bfloat16),
        "w_query": noise(key_list[6], (D, Q_WIDTH), D ** -0.5, 0.125, ((0, 32),)),
        "w_key": noise(key_list[7], (D, KV_WIDTH), D ** -0.5, 0.125, ((0, 32),)),
        "w_value": noise(key_list[8], (D, KV_WIDTH), D ** -0.5, 0.125, ((0, 32),)),
        "query_gain": jnp.clip(1.0 + 0.18 * jax.random.normal(key_list[9], (HEAD_DIM,), jnp.float32), 0.099609375, 1.8984375).astype(jnp.bfloat16),
        "key_gain": jnp.clip(1.0 + 0.18 * jax.random.normal(key_list[10], (HEAD_DIM,), jnp.float32), 0.099609375, 1.8984375).astype(jnp.bfloat16),
        "w_out": noise(key_list[11], (Q_WIDTH, D), (Q_WIDTH // 64) ** -0.5, 1.25, ((0, 32),)),
        "ffn_gain": jnp.clip(1.0 + 0.1 * jax.random.normal(key_list[12], (D,), jnp.float32), 0.5, 1.5).astype(jnp.bfloat16),
        "w_gate": noise(key_list[13], (D, FF), D ** -0.5, 0.125, ((0, 32),)),
        "w_up": noise(key_list[14], (D, FF), D ** -0.5, 0.125, ((0, 32),)),
        "w_down": noise(key_list[15], (FF, D), FF ** -0.5, 0.09375, ((0, 32),)),
    }


eps = 1e-06

@jax.custom_vjp
def low(v):
    return lax.optimization_barrier(v.astype(jnp.bfloat16)).astype(jnp.float32)

@jax.custom_vjp
def low_back(v):
    return v

def low_keep(v):
    return (low(v), None)

def low_pass(kept, grad):
    return (grad,)

def back_keep(v):
    return (v, None)

def back_low(kept, grad):
    return (low(grad),)
low.defvjp(low_keep, low_pass)
low_back.defvjp(back_keep, back_low)

def matmul(left, right):
    return jnp.dot(left, right, precision=lax.Precision.HIGHEST, preferred_element_type=jnp.float32)

def rms_scale(values_in, scale_gain):
    return values_in * lax.rsqrt(lax.optimization_barrier(jnp.mean(values_in * values_in, axis=-1, keepdims=True)) + eps) * scale_gain

def rotary(positions):
    half_dim = HEAD_DIM // 2
    frequency = jnp.exp(jnp.arange(half_dim, dtype=jnp.float32) * (-2.0 * math.log(10000.0) / HEAD_DIM))
    angles = positions.astype(jnp.float32)[:, None] * frequency[None, :]
    return (jnp.cos(angles)[:, None, :], jnp.sin(angles)[:, None, :])

def rotate(values_in, cosine, sine):
    half_dim = values_in.shape[-1] // 2
    first_half = values_in[..., :half_dim]
    second_half = values_in[..., half_dim:]
    return jnp.concatenate([first_half * cosine - second_half * sine, second_half * cosine + first_half * sine], axis=-1)

def attend(query, keys, values, doc_row):
    length = query.shape[0]
    block_rows = min(QROWS, length)
    blocks = length // block_rows
    query_blocks = query.reshape(blocks, block_rows, HEADS, HEAD_DIM)
    doc_blocks = doc_row.reshape(blocks, block_rows)
    key_positions = jnp.arange(length, dtype=jnp.int32)
    position_blocks = key_positions.reshape(blocks, block_rows)

    def one_block(items):
        query_part, doc_part, position_part = items
        raw_scores = jnp.einsum('qhd,khd->hqk', query_part, keys, precision=lax.Precision.HIGHEST)
        scores = low_back(0.125 * raw_scores)
        allowed = (key_positions[None, :] <= position_part[:, None]) & (doc_row[None, :] == doc_part[:, None])
        masked = jnp.where(allowed[None], scores, -1e+30)
        row_max = lax.optimization_barrier(jnp.max(masked, axis=-1, keepdims=True))
        exp_scores = jnp.exp(masked - row_max)
        attn_probs = low(exp_scores / lax.optimization_barrier(jnp.sum(exp_scores, axis=-1, keepdims=True)))
        return jnp.einsum('hqk,khd->qhd', attn_probs, values, precision=lax.Precision.HIGHEST)
    mixed = lax.map(jax.checkpoint(one_block), (query_blocks, doc_blocks, position_blocks))
    return mixed.reshape(length, HEADS, HEAD_DIM)

def layer(inputs_f, weights, doc_row):
    attn_gain, w_query, w_key, w_value, query_gain, key_gain, w_out, ffn_gain, w_gate, w_up, w_down = weights
    length = inputs_f.shape[0]
    group_size = HEADS // KV_HEADS
    cosine, sine = rotary(jnp.arange(length, dtype=jnp.int32))
    normed = low(rms_scale(inputs_f, attn_gain))
    query_lin = low_back(matmul(normed, w_query)).reshape(length, HEADS, HEAD_DIM)
    key_lin = low_back(matmul(normed, w_key)).reshape(length, KV_HEADS, HEAD_DIM)
    value_lin = low_back(matmul(normed, w_value)).reshape(length, KV_HEADS, HEAD_DIM)
    query = low_back(low(rotate(rms_scale(query_lin, query_gain), cosine, sine)))
    keys = low(rotate(rms_scale(key_lin, key_gain), cosine, sine))
    keys = low_back(jnp.repeat(keys, group_size, axis=1))
    values = low_back(jnp.repeat(low(value_lin), group_size, axis=1))
    mixed = low_back(low(attend(query, keys, values, doc_row))).reshape(length, Q_WIDTH)
    resid = inputs_f + low_back(matmul(mixed, w_out))
    normed_ffn = low(rms_scale(resid, ffn_gain))
    gate_lin = low_back(matmul(normed_ffn, w_gate))
    up_lin = low_back(matmul(normed_ffn, w_up))
    hidden = low(jax.nn.silu(gate_lin) * up_lin)
    return resid + low_back(matmul(hidden, w_down))

def reference(tokens, out_grad, doc_ids, corpus, corpus_weight, attn_gain, w_query, w_key, w_value, query_gain, key_gain, w_out, ffn_gain, w_gate, w_up, w_down):
    params = tuple((weight_in.astype(jnp.float32) for weight_in in (attn_gain, w_query, w_key, w_value, query_gain, key_gain, w_out, ffn_gain, w_gate, w_up, w_down)))
    tag_range = jnp.arange(TAGS, dtype=jnp.int32)

    def step(totals, items):
        inputs_b, cotangent, doc_row, corpus_tag = items
        scale = jnp.sum(jnp.where(tag_range == corpus_tag, corpus_weight, jnp.zeros_like(corpus_weight)))

        def forward(inputs_f, weights):
            return layer(inputs_f, weights, doc_row)
        result, backward = jax.vjp(forward, inputs_b.astype(jnp.float32), params)
        grad_inputs, grad_weights = backward(scale * cotangent.astype(jnp.float32))
        totals = tuple((older + newer for older, newer in zip(totals, grad_weights)))
        return (totals, (result.astype(jnp.bfloat16), grad_inputs.astype(jnp.bfloat16)))
    initial = tuple((jnp.zeros(weight_in.shape, jnp.float32) for weight_in in params))
    totals, outputs = lax.scan(step, initial, (tokens, out_grad, doc_ids, corpus))
    layer_out, tokens_grad = outputs
    return (layer_out, tokens_grad, totals[0], totals[1], totals[2], totals[3], totals[4], totals[5], totals[6], totals[7], totals[8], totals[9], totals[10])
```

```python
import functools
import math

import jax
import jax.numpy as jnp
import numpy as np
from jax import lax
from jax.experimental import pallas as pl
from jax.experimental.pallas import tpu as pltpu
from jax.sharding import Mesh
from jax.sharding import PartitionSpec as P

HEADS = 20
KV_HEADS = 5
GROUP = HEADS // KV_HEADS
HEAD_DIM = 64
TAGS = 4
Q_WIDTH = HEADS * HEAD_DIM
KV_WIDTH = KV_HEADS * HEAD_DIM
DOC_MOST = 1024
Z_CHIPS = 4
EPS = 1e-06
SCORE_SCALE = 0.125
LOG2E = math.log2(math.e)
MASKED = -1e30
KEY_BLOCK = 256

bf16 = jnp.bfloat16
f32 = jnp.float32


def dot(left, right, left_dim, right_dim):
    return lax.dot_general(
        left, right, (((left_dim,), (right_dim,)), ((), ())), preferred_element_type=f32
    )


def matmul(left, right):
    return dot(left, right, 1, 0)


def forward_kernel(meta, start_ref, q_ref, k_ref, v_ref, o_ref, lse_ref, bias_ref, q_rows, v_rows, acc):
    rows = q_ref.shape[1]
    window = k_ref.shape[1]
    low, high, q_start = meta[0], meta[1], meta[2]

    @pl.when(pl.program_id(0) == 0)
    def _():
        q_pos = q_start + lax.broadcasted_iota(jnp.int32, (rows, KEY_BLOCK), 0)
        lanes = lax.broadcasted_iota(jnp.int32, (rows, KEY_BLOCK), 1)

        def fill(block, carry):
            key_pos = block * KEY_BLOCK + lanes
            allowed = (key_pos >= start_ref[...]) & (key_pos <= q_pos)
            bias_ref[block] = jnp.where(allowed, 0.0, MASKED)
            return carry

        lax.fori_loop(low, high, fill, 0)

    q_cols = q_ref[...].T
    for head in range(GROUP):
        q_rows[head] = q_cols[:, head * HEAD_DIM : (head + 1) * HEAD_DIM]
    sub = lax.broadcasted_iota(jnp.int32, (HEAD_DIM, window), 0)
    ones = jnp.where(sub == 0, 1.0, 0.0).astype(bf16)
    v_rows[...] = jnp.concatenate([v_ref[...], ones], axis=0).T
    acc[...] = jnp.zeros_like(acc)

    def body(block, carry):
        at = pl.multiple_of(block * KEY_BLOCK, KEY_BLOCK)
        key_cols = k_ref[:, pl.ds(at, KEY_BLOCK)]
        value_rows = v_rows[pl.ds(at, KEY_BLOCK), :]
        bias = bias_ref[block]
        for head in range(GROUP):
            raw = jnp.dot(q_rows[head], key_cols, preferred_element_type=f32)
            probs = jnp.exp2(raw * (SCORE_SCALE * LOG2E) + bias).astype(bf16)
            acc[head] += jnp.dot(probs, value_rows, preferred_element_type=f32)
        return carry

    lax.fori_loop(low, high, body, 0)
    for head in range(GROUP):
        turned = acc[head].T
        total = turned[HEAD_DIM : HEAD_DIM + 1, :]
        o_ref[head * HEAD_DIM : (head + 1) * HEAD_DIM, :] = (turned[:HEAD_DIM] / total).astype(bf16)
        lse_ref[0, head : head + 1, :] = jnp.log2(total)


def backward_kernel(
    meta, start_ref, q_ref, k_ref, v_ref, go_ref, o_ref, lse_ref,
    dq_ref, dk_ref, dv_ref, bias_ref, q_rows, go_rows, k_rows, v_rows, dq_acc, delta_ref,
):
    rows = q_ref.shape[1]
    low, high, q_start = meta[0], meta[1], meta[2]

    @pl.when(pl.program_id(0) == 0)
    def _():
        q_pos = q_start + lax.broadcasted_iota(jnp.int32, (KEY_BLOCK, rows), 1)
        subs = lax.broadcasted_iota(jnp.int32, (KEY_BLOCK, rows), 0)

        def fill(block, carry):
            key_pos = block * KEY_BLOCK + subs
            allowed = (key_pos >= start_ref[...]) & (key_pos <= q_pos)
            bias_ref[block] = jnp.where(allowed, 0.0, MASKED)
            return carry

        lax.fori_loop(low, high, fill, 0)

    q_cols = q_ref[...].T
    go_cols = go_ref[...].T
    for head in range(GROUP):
        part = slice(head * HEAD_DIM, (head + 1) * HEAD_DIM)
        q_rows[head] = q_cols[:, part]
        go_rows[head] = go_cols[:, part]
        delta_ref[head : head + 1, :] = jnp.sum(
            go_ref[part, :].astype(f32) * o_ref[part, :].astype(f32), axis=0, keepdims=True
        )
    k_rows[...] = k_ref[...].T
    v_rows[...] = v_ref[...].T
    dk_ref[...] = jnp.zeros_like(dk_ref)
    dv_ref[...] = jnp.zeros_like(dv_ref)
    dq_acc[...] = jnp.zeros_like(dq_acc)

    def body(block, carry):
        at = pl.multiple_of(block * KEY_BLOCK, KEY_BLOCK)
        key_cols = k_ref[:, pl.ds(at, KEY_BLOCK)]
        key_rows = k_rows[pl.ds(at, KEY_BLOCK), :]
        value_rows = v_rows[pl.ds(at, KEY_BLOCK), :]
        bias = bias_ref[block]
        dk = jnp.zeros((KEY_BLOCK, HEAD_DIM), f32)
        dv = jnp.zeros((KEY_BLOCK, HEAD_DIM), f32)
        for head in range(GROUP):
            part = slice(head * HEAD_DIM, (head + 1) * HEAD_DIM)
            raw = jnp.dot(key_rows, q_ref[part, :], preferred_element_type=f32)
            probs = jnp.exp2(
                raw * (SCORE_SCALE * LOG2E) + (bias - lse_ref[0, head : head + 1, :])
            )
            grad_probs = jnp.dot(value_rows, go_ref[part, :], preferred_element_type=f32)
            grad_scores = (probs * (grad_probs - delta_ref[head : head + 1, :])).astype(bf16)
            dv += jnp.dot(probs.astype(bf16), go_rows[head], preferred_element_type=f32)
            dk += jnp.dot(grad_scores, q_rows[head], preferred_element_type=f32)
            dq_acc[part, :] += jnp.dot(key_cols, grad_scores, preferred_element_type=f32)
        dk_ref[:, pl.ds(at, KEY_BLOCK)] = (SCORE_SCALE * dk).T.astype(bf16)
        dv_ref[:, pl.ds(at, KEY_BLOCK)] = dv.T.astype(bf16)
        return carry

    lax.fori_loop(low, high, body, 0)
    dq_ref[...] = (SCORE_SCALE * dq_acc[...]).astype(bf16)


def attend_forward(meta, start_col, q_t, kv_t):
    rows, window = q_t.shape[1], kv_t.shape[1]
    wide = GROUP * HEAD_DIM
    return pl.pallas_call(
        forward_kernel,
        name="attend_forward",
        grid_spec=pltpu.PrefetchScalarGridSpec(
            num_scalar_prefetch=1,
            grid=(KV_HEADS,),
            in_specs=[
                pl.BlockSpec((rows, 1), lambda g, m: (0, 0)),
                pl.BlockSpec((wide, rows), lambda g, m: (g, 0)),
                pl.BlockSpec((HEAD_DIM, window), lambda g, m: (g, 0)),
                pl.BlockSpec((HEAD_DIM, window), lambda g, m: (KV_HEADS + g, 0)),
            ],
            out_specs=[
                pl.BlockSpec((wide, rows), lambda g, m: (g, 0)),
                pl.BlockSpec((1, GROUP, rows), lambda g, m: (g, 0, 0)),
            ],
            scratch_shapes=[
                pltpu.VMEM((window // KEY_BLOCK, rows, KEY_BLOCK), f32),
                pltpu.VMEM((GROUP, rows, HEAD_DIM), bf16),
                pltpu.VMEM((window, 2 * HEAD_DIM), bf16),
                pltpu.VMEM((GROUP, rows, 2 * HEAD_DIM), f32),
            ],
        ),
        out_shape=[
            jax.ShapeDtypeStruct((Q_WIDTH, rows), bf16),
            jax.ShapeDtypeStruct((KV_HEADS, GROUP, rows), f32),
        ],
        cost_estimate=pl.CostEstimate(
            flops=4 * HEADS * rows * window * 128, bytes_accessed=4 * 1024 * 1024,
            transcendentals=HEADS * rows * window,
        ),
    )(meta, start_col, q_t, kv_t, kv_t)


def attend_backward(meta, start_row, q_t, kv_t, go_t, o_t, lse):
    rows, window = q_t.shape[1], kv_t.shape[1]
    wide = GROUP * HEAD_DIM
    return pl.pallas_call(
        backward_kernel,
        name="attend_backward",
        grid_spec=pltpu.PrefetchScalarGridSpec(
            num_scalar_prefetch=1,
            grid=(KV_HEADS,),
            in_specs=[
                pl.BlockSpec((1, rows), lambda g, m: (0, 0)),
                pl.BlockSpec((wide, rows), lambda g, m: (g, 0)),
                pl.BlockSpec((HEAD_DIM, window), lambda g, m: (g, 0)),
                pl.BlockSpec((HEAD_DIM, window), lambda g, m: (KV_HEADS + g, 0)),
                pl.BlockSpec((wide, rows), lambda g, m: (g, 0)),
                pl.BlockSpec((wide, rows), lambda g, m: (g, 0)),
                pl.BlockSpec((1, GROUP, rows), lambda g, m: (g, 0, 0)),
            ],
            out_specs=[
                pl.BlockSpec((wide, rows), lambda g, m: (g, 0)),
                pl.BlockSpec((HEAD_DIM, window), lambda g, m: (g, 0)),
                pl.BlockSpec((HEAD_DIM, window), lambda g, m: (g, 0)),
            ],
            scratch_shapes=[
                pltpu.VMEM((window // KEY_BLOCK, KEY_BLOCK, rows), f32),
                pltpu.VMEM((GROUP, rows, HEAD_DIM), bf16),
                pltpu.VMEM((GROUP, rows, HEAD_DIM), bf16),
                pltpu.VMEM((window, HEAD_DIM), bf16),
                pltpu.VMEM((window, HEAD_DIM), bf16),
                pltpu.VMEM((wide, rows), f32),
                pltpu.VMEM((8, rows), f32),
            ],
        ),
        out_shape=[
            jax.ShapeDtypeStruct((Q_WIDTH, rows), bf16),
            jax.ShapeDtypeStruct((KV_WIDTH, window), bf16),
            jax.ShapeDtypeStruct((KV_WIDTH, window), bf16),
        ],
        cost_estimate=pl.CostEstimate(
            flops=10 * HEADS * rows * window * 128, bytes_accessed=8 * 1024 * 1024,
            transcendentals=HEADS * rows * window,
        ),
    )(meta, start_row, q_t, kv_t, kv_t, go_t, o_t, lse)


class Transfers:
    def __init__(self, sizes):
        self.sizes = sizes

    def shift(self, value, axis, step):
        size = self.sizes[axis]
        return lax.ppermute(value, axis, [(i, (i + step) % size) for i in range(size)])

    def place(self, pieces, axis, dim):
        size = self.sizes[axis]
        if size == 1:
            return jnp.expand_dims(pieces[0], dim)
        shape = pieces[0].shape
        rank = len(shape) + 1
        index = lax.broadcasted_iota(
            jnp.int32, tuple(size if d == dim else 1 for d in range(rank)), dim
        )
        back = jnp.mod(lax.axis_index(axis) - index, size)
        whole = jnp.broadcast_to(
            jnp.expand_dims(pieces[0], dim), shape[:dim] + (size,) + shape[dim:]
        )
        for k in range(1, size):
            whole = jnp.where(back == k, jnp.expand_dims(pieces[k], dim), whole)
        return whole

    def ring(self, value, axis):
        pieces = [value]
        for _ in range(1, self.sizes[axis]):
            pieces.append(self.shift(pieces[-1], axis, 1))
        return pieces

    def gather(self, value, axis, dim):
        return self.place(self.ring(value, axis), axis, dim)

    def take(self, value, axis, dim, step):
        size = self.sizes[axis]
        index = jnp.mod(lax.axis_index(axis) + step, size)
        return lax.dynamic_index_in_dim(value, index, dim, keepdims=False)

    def scatter(self, value, axis, dim):
        total = self.take(value, axis, dim, 0).astype(f32)
        for k in range(1, self.sizes[axis]):
            sent = self.take(value, axis, dim, k).astype(bf16)
            total = total + self.shift(sent, axis, k).astype(f32)
        return total

    def exchange(self, value, axis, dim, out_dim):
        pieces = [self.take(value, axis, dim, 0)]
        for k in range(1, self.sizes[axis]):
            pieces.append(self.shift(self.take(value, axis, dim, k), axis, k))
        return self.place(pieces, axis, out_dim)

    def gather_chips(self, value, order):
        have = []
        for axis in order:
            dim = sum(1 for a in have if "ycz x".index(a) < "ycz x".index(axis))
            value = self.gather(value, axis, dim)
            have.append(axis)
        return value

    def scatter_chips(self, value, order):
        have = ["y", "c", "z", "x"]
        for number, axis in enumerate(order):
            value = self.scatter(value, axis, have.index(axis))
            if number < len(order) - 1:
                value = value.astype(bf16)
            have.remove(axis)
        return value


def head_forward(lin, gain, cosine, sine):
    scale = lax.rsqrt(jnp.mean(lin * lin, axis=1, keepdims=True) + EPS)
    normal = lin * scale * gain[None, :, None]
    half = HEAD_DIM // 2
    first, second = normal[:, :half], normal[:, half:]
    turned = jnp.concatenate(
        [first * cosine - second * sine, second * cosine + first * sine], axis=1
    )
    return turned, scale


def head_backward(grad, lin, scale, gain, cosine, sine):
    half = HEAD_DIM // 2
    first, second = grad[:, :half], grad[:, half:]
    back = jnp.concatenate(
        [first * cosine + second * sine, second * cosine - first * sine], axis=1
    )
    gain_grad = jnp.sum(back * lin * scale, axis=(0, 2))
    scaled = back * gain[None, :, None]
    lin_grad = scale * scaled - lin * (scale**3) * jnp.mean(scaled * lin, axis=1, keepdims=True)
    return lin_grad, gain_grad


def row_scale(values):
    return lax.rsqrt(jnp.mean(values * values, axis=-1, keepdims=True) + EPS)


def norm_backward(grad, values, scale):
    return scale * grad - values * (scale**3) * jnp.mean(grad * values, axis=-1, keepdims=True)


def per_device(
    sizes, tokens, out_grad, doc_ids, corpus, corpus_weight, attn_gain, w_query, w_key, w_value,
    query_gain, key_gain, w_out, ffn_gain, w_gate, w_up, w_down,
):
    move = Transfers(sizes)
    ys, cs, zs, xs = (sizes[a] for a in "yczx")
    batches, local, width = tokens.shape
    span = xs * local
    back_groups = -(-(DOC_MOST - 1) // span)
    window = (back_groups + 1) * span
    at_z, at_x = lax.axis_index("z"), lax.axis_index("x")
    ffn_part = w_gate.shape[1] // (ys * cs)
    d_rows = w_gate.shape[0]

    gain_a = attn_gain.astype(f32)[:, None]
    gain_f = ffn_gain.astype(f32)[:, None]
    w_qkv = jnp.concatenate([w_key, w_value, w_query], axis=1)
    w_qkv_low = (w_qkv.astype(f32) * gain_a).astype(bf16)

    def gather_weight(shard):
        half = shard.shape[1] // 2
        near = move.gather(shard, "z", 0)
        first, second = near[..., :half], near[..., half:]
        first = move.gather(move.gather(first, "y", 0), "x", 2)
        second = move.gather(move.gather(second, "x", 1), "y", 0)
        return tuple(
            move.gather(part, "c", 1).reshape(-1, half) for part in (first, second)
        )

    w_qkv_a, w_qkv_b = gather_weight(w_qkv_low)
    w_out_a, w_out_b = gather_weight(w_out)

    w_gate_low = (w_gate.astype(f32) * gain_f).astype(bf16).reshape(d_rows, ys, cs, 1, ffn_part)
    w_up_low = (w_up.astype(f32) * gain_f).astype(bf16).reshape(d_rows, ys, cs, 1, ffn_part)
    both = jnp.concatenate([w_gate_low, w_up_low], axis=3).reshape(d_rows, ys, cs, 2 * ffn_part)
    both = move.exchange(both, "c", 2, 0)
    both = move.exchange(both, "y", 2, 0)
    both = move.gather(both, "z", 2)
    w_both = move.gather(both, "x", 3).reshape(width, 2 * ffn_part)
    w_down_all = move.gather(move.gather(w_down, "x", 0), "z", 0).reshape(ffn_part, width)

    group_docs = move.gather(doc_ids, "x", 1).reshape(batches, span)
    doc_groups = [group_docs]
    for k in range(1, back_groups + 1):
        earlier = move.shift(doc_groups[-1], "z", 1)
        doc_groups.append(earlier)
    doc_window = jnp.concatenate(
        [
            jnp.where(at_z >= k, doc_groups[k], -1)
            for k in range(back_groups, -1, -1)
        ],
        axis=1,
    )
    starts = jnp.sum(
        (doc_window[:, None, :] < doc_ids[:, :, None]).astype(jnp.int32), axis=-1
    )
    q_start = back_groups * span + at_x * local
    high = (q_start + local + KEY_BLOCK - 1) // KEY_BLOCK

    half_dim = HEAD_DIM // 2
    frequency = jnp.exp(
        jnp.arange(half_dim, dtype=f32) * (-2.0 * math.log(10000.0) / HEAD_DIM)
    )
    positions = (at_z * xs + at_x) * local + jnp.arange(local, dtype=jnp.int32)
    angles = frequency[:, None] * positions.astype(f32)[None, :]
    cosine, sine = jnp.cos(angles)[None], jnp.sin(angles)[None]
    gain_q, gain_k = query_gain.astype(f32), key_gain.astype(f32)

    tag_range = jnp.arange(TAGS, dtype=jnp.int32)
    inputs = [tokens[b].astype(f32) for b in range(batches)]
    grads_out = [
        jnp.sum(jnp.where(tag_range == corpus[b], corpus_weight, 0.0)) * out_grad[b].astype(f32)
        for b in range(batches)
    ]

    def seq_gather(rows):
        chips = jnp.concatenate(move.ring(rows, "y"), axis=0)
        return jnp.concatenate(move.ring(chips, "c"), axis=0)

    def seq_scatter(partial):
        blocks = partial.reshape(cs, ys, local, width)
        total = blocks[0].astype(f32)
        for k in range(1, cs):
            total = total + move.shift(blocks[k], "c", -k).astype(f32)
        result = total[0]
        for k in range(1, ys):
            result = result + move.shift(total[k].astype(bf16), "y", -k).astype(f32)
        return result

    grads_all = [seq_gather(g.astype(bf16)) for g in grads_out]

    state = []
    for b in range(batches):
        scale_in = row_scale(inputs[b])
        normed = (inputs[b] * scale_in).astype(bf16)
        lin_a = dot(w_qkv_a, normed, 0, 1)
        lin_b = dot(w_qkv_b, normed, 0, 1)
        key_lin = lin_a[:KV_WIDTH].reshape(KV_HEADS, HEAD_DIM, local)
        value_t = lin_a[KV_WIDTH : 2 * KV_WIDTH].astype(bf16)
        query_lin = jnp.concatenate([lin_a[2 * KV_WIDTH :], lin_b], axis=0).reshape(
            HEADS, HEAD_DIM, local
        )
        key_rot, key_scale = head_forward(key_lin, gain_k, cosine, sine)
        query_rot, query_scale = head_forward(query_lin, gain_q, cosine, sine)
        query_t = query_rot.astype(bf16).reshape(Q_WIDTH, local)
        kv = jnp.concatenate([key_rot.astype(bf16).reshape(KV_WIDTH, local), value_t], axis=0)
        kv_groups = [move.gather(kv, "x", 1).reshape(2 * KV_WIDTH, span)]
        for k in range(back_groups):
            kv_groups.append(move.shift(kv_groups[-1], "z", 1))
        kv_t = jnp.concatenate(kv_groups[::-1], axis=1)
        meta = jnp.stack([starts[b, 0] // KEY_BLOCK, high, q_start]).astype(jnp.int32)
        mixed_t, lse = attend_forward(meta, starts[b][:, None], query_t, kv_t)
        resid = inputs[b] + jnp.concatenate(
            [dot(mixed_t, w_out_a, 0, 0), dot(mixed_t, w_out_b, 0, 0)], axis=1
        )
        scale_mid = row_scale(resid)
        normed2_all = seq_gather((resid * scale_mid).astype(bf16))
        state.append(
            dict(
                scale_in=scale_in, normed=normed, key_lin=key_lin, query_lin=query_lin,
                key_scale=key_scale, query_scale=query_scale, query_t=query_t, kv_t=kv_t,
                meta=meta, mixed_t=mixed_t, lse=lse, resid=resid, scale_mid=scale_mid,
                normed2_all=normed2_all,
            )
        )

    outputs = []
    grad_both_wide = None
    grad_down_wide = None
    for b in range(batches):
        s = state[b]
        wide = matmul(s["normed2_all"], w_both)
        gate, up = wide[:, :ffn_part], wide[:, ffn_part:]
        sig = jax.nn.sigmoid(gate)
        silu = gate * sig
        hidden = (silu * up).astype(bf16)
        grad_hidden = dot(grads_all[b], w_down_all, 1, 1)
        grad_gate = (grad_hidden * up * (sig * (1.0 + gate * (1.0 - sig)))).astype(bf16)
        grad_up = (grad_hidden * silu).astype(bf16)
        grad_wide = jnp.concatenate([grad_gate, grad_up], axis=1)
        grad_normed2 = seq_scatter(dot(grad_wide, w_both, 1, 1).astype(bf16))
        grad_resid = grads_out[b] + norm_backward(grad_normed2, s["resid"], s["scale_mid"])
        s["grad_resid"] = grad_resid
        s["grad_resid_low"] = grad_resid.astype(bf16)
        down = dot(hidden, grads_all[b], 0, 0)
        grad_down_wide = down if b == 0 else grad_down_wide + down
        part = dot(s["normed2_all"], grad_wide, 0, 0)
        grad_both_wide = part if b == 0 else grad_both_wide + part
        outputs.append(
            (s["resid"] + seq_scatter(matmul(hidden, w_down_all).astype(bf16))).astype(bf16)
        )

    down_parts = grad_down_wide.astype(bf16).reshape(zs, xs, -1, width)
    grad_down = move.scatter(move.scatter(down_parts, "x", 1).astype(bf16), "z", 0)
    both_parts = grad_both_wide.astype(bf16).reshape(ys, cs, zs, xs, d_rows, 2 * ffn_part)
    both_sum = move.scatter(move.scatter(both_parts, "x", 3).astype(bf16), "z", 2).astype(bf16)
    both_sum = move.exchange(both_sum, "y", 0, 2)
    both_sum = move.exchange(both_sum, "c", 0, 2).astype(f32)
    grad_gate_w = both_sum[..., :ffn_part].reshape(d_rows, -1)
    grad_up_w = both_sum[..., ffn_part:].reshape(d_rows, -1)

    gq_parts, gq_gain, gk_gain, token_grads = [], 0.0, 0.0, []
    qkv_grads = []
    for b in range(batches):
        s = state[b]
        low_grad = s["grad_resid_low"]
        grad_mixed_t = jnp.concatenate(
            [dot(w_out_a, low_grad[:, : width // 2], 1, 1)], axis=0
        ) + dot(w_out_b, low_grad[:, width // 2 :], 1, 1)
        grad_mixed_t = grad_mixed_t.astype(bf16)
        dq_t, dk_t, dv_t = attend_backward(
            s["meta"], starts[b][None, :], s["query_t"], s["kv_t"], grad_mixed_t, s["mixed_t"],
            s["lse"],
        )
        dkv = jnp.concatenate([dk_t, dv_t], axis=0).reshape(
            2 * KV_WIDTH, back_groups + 1, span
        )
        carried = dkv[:, 0]
        for k in range(1, back_groups + 1):
            carried = (
                move.shift(carried.astype(bf16), "z", -1).astype(f32) + dkv[:, k].astype(f32)
            )
        carried = carried.astype(bf16).reshape(2 * KV_WIDTH, xs, local)
        dkv_sum = move.scatter(carried, "x", 1)
        key_grad, key_gain_part = head_backward(
            dkv_sum[:KV_WIDTH].reshape(KV_HEADS, HEAD_DIM, local), s["key_lin"], s["key_scale"],
            gain_k, cosine, sine,
        )
        query_grad, query_gain_part = head_backward(
            dq_t.astype(f32).reshape(HEADS, HEAD_DIM, local), s["query_lin"], s["query_scale"],
            gain_q, cosine, sine,
        )
        gq_gain = gq_gain + query_gain_part
        gk_gain = gk_gain + key_gain_part
        query_grad = query_grad.astype(bf16).reshape(Q_WIDTH, local)
        grad_a = jnp.concatenate(
            [
                key_grad.astype(bf16).reshape(KV_WIDTH, local),
                dkv_sum[KV_WIDTH:].astype(bf16),
                query_grad[:KV_WIDTH],
            ],
            axis=0,
        )
        grad_b = query_grad[KV_WIDTH:]
        qkv_grads.append((grad_a, grad_b))
        grad_normed = dot(grad_a, w_qkv_a, 0, 1) + dot(grad_b, w_qkv_b, 0, 1)
        token_grads.append(
            (s["grad_resid"] + norm_backward(grad_normed, inputs[b], s["scale_in"])).astype(bf16)
        )

    def scatter_weight(first, second, rows):
        parts = []
        for part, order in ((first, "cxyz"), (second, "cyxz")):
            shaped = part.astype(bf16).reshape(ys, cs, zs, xs, rows, -1)
            parts.append(move.scatter_chips(shaped, order))
        return jnp.concatenate(parts, axis=1)

    normed_all = jnp.concatenate([s["normed"] for s in state], axis=0)
    mixed_all = jnp.concatenate([s["mixed_t"] for s in state], axis=1)
    low_all = jnp.concatenate([s["grad_resid_low"] for s in state], axis=0)
    grad_out_w = scatter_weight(
        matmul(mixed_all, low_all[:, : width // 2]),
        matmul(mixed_all, low_all[:, width // 2 :]),
        w_out.shape[0],
    )
    grad_qkv = scatter_weight(
        dot(normed_all, jnp.concatenate([g[0] for g in qkv_grads], axis=1), 0, 1),
        dot(normed_all, jnp.concatenate([g[1] for g in qkv_grads], axis=1), 0, 1),
        d_rows,
    )

    attn_gain_grad = jnp.sum(grad_qkv * w_qkv.astype(f32), axis=1)
    ffn_gain_grad = jnp.sum(
        grad_gate_w * w_gate.astype(f32) + grad_up_w * w_up.astype(f32), axis=1
    )
    grad_qkv = grad_qkv * gain_a
    small = jnp.concatenate([gq_gain, gk_gain])[None, :]
    for axis in "cyxz":
        small = jnp.sum(move.gather(small, axis, 0), axis=0)

    return (
        jnp.stack(outputs),
        jnp.stack(token_grads),
        attn_gain_grad,
        grad_qkv[:, 2 * KV_WIDTH :],
        grad_qkv[:, :KV_WIDTH],
        grad_qkv[:, KV_WIDTH : 2 * KV_WIDTH],
        small[0, :HEAD_DIM],
        small[0, HEAD_DIM:],
        grad_out_w,
        ffn_gain_grad,
        grad_gate_w * gain_f,
        grad_up_w * gain_f,
        grad_down,
    )


def solution(mesh):
    sizes = {"c": 2, "z": Z_CHIPS}
    sizes["y"] = mesh.shape["seq"] // sizes["c"]
    sizes["x"] = mesh.shape["ctx"] // sizes["z"]
    grid = Mesh(mesh.devices.reshape([sizes[a] for a in "yczx"]), ("y", "c", "z", "x"))
    seq, ctx, every = ("y", "c"), ("z", "x"), ("y", "c", "z", "x")
    acts, vector, matrix = P(seq, ctx, None), P(every), P(every, None)
    in_specs = (
        acts, acts, P(seq, ctx), P(seq), P(), vector, matrix, matrix, matrix, P(), P(), matrix,
        vector, matrix, matrix, matrix,
    )
    out_specs = (
        acts, acts, vector, matrix, matrix, matrix, P(), P(), matrix, vector, matrix, matrix,
        matrix,
    )
    return jax.shard_map(
        functools.partial(per_device, sizes), mesh=grid, in_specs=in_specs, out_specs=out_specs,
        check_vma=False,
    )
```

```python
import functools
import math

import jax
import jax.numpy as jnp
import numpy as np
from jax import lax
from jax.experimental import pallas as pl
from jax.experimental.pallas import tpu as pltpu
from jax.sharding import Mesh
from jax.sharding import PartitionSpec as P

HEADS = 20
KV_HEADS = 5
GROUP = HEADS // KV_HEADS
HEAD_DIM = 64
TAGS = 4
Q_WIDTH = HEADS * HEAD_DIM
KV_WIDTH = KV_HEADS * HEAD_DIM
DOC_MOST = 1024
Z_CHIPS = 4
EPS = 1e-06
SCORE_SCALE = 0.125
LOG2E = math.log2(math.e)
MASKED = -1e30

bf16 = jnp.bfloat16
f32 = jnp.float32


def dot(left, right, left_dim, right_dim):
    return lax.dot_general(
        left, right, (((left_dim,), (right_dim,)), ((), ())), preferred_element_type=f32
    )


def matmul(left, right):
    return dot(left, right, 1, 0)


def block_slot(block, at_x, xs):
    return (block // xs) * xs + lax.rem(at_x - lax.rem(block, xs) + xs, xs)


def forward_kernel(xs, meta, start_ref, q_ref, k_ref, v_ref, o_ref, lse_ref, bias_ref, q_rows, acc):
    rows = q_ref.shape[1]
    size = k_ref.shape[2]
    low, high, q_start, at_x = meta[0], meta[1], meta[2], meta[3]

    @pl.when(pl.program_id(0) == 0)
    def _():
        q_pos = q_start + lax.broadcasted_iota(jnp.int32, (rows, size), 0)
        lanes = lax.broadcasted_iota(jnp.int32, (rows, size), 1)

        def fill(block, carry):
            key_pos = block * size + lanes
            allowed = (key_pos >= start_ref[...]) & (key_pos <= q_pos)
            bias_ref[block] = jnp.where(allowed, 0.0, MASKED)
            return carry

        lax.fori_loop(low, high, fill, 0)

    q_cols = q_ref[...].T
    for head in range(GROUP):
        q_rows[head] = q_cols[:, head * HEAD_DIM : (head + 1) * HEAD_DIM]
    sub = lax.broadcasted_iota(jnp.int32, (HEAD_DIM, size), 0)
    ones = jnp.where(sub == 0, 1.0, 0.0).astype(bf16)
    acc[...] = jnp.zeros_like(acc)

    def body(block, carry):
        slot = block_slot(block, at_x, xs)
        key_cols = k_ref[slot]
        value_rows = jnp.concatenate([v_ref[slot], ones], axis=0).T
        bias = bias_ref[block]
        for head in range(GROUP):
            raw = jnp.dot(q_rows[head], key_cols, preferred_element_type=f32)
            probs = jnp.exp2(raw * (SCORE_SCALE * LOG2E) + bias).astype(bf16)
            acc[head] += jnp.dot(probs, value_rows, preferred_element_type=f32)
        return carry

    lax.fori_loop(low, high, body, 0)
    for head in range(GROUP):
        turned = acc[head].T
        total = turned[HEAD_DIM : HEAD_DIM + 1, :]
        o_ref[head * HEAD_DIM : (head + 1) * HEAD_DIM, :] = (turned[:HEAD_DIM] / total).astype(bf16)
        lse_ref[0, head : head + 1, :] = jnp.log2(total)


def backward_kernel(
    xs, meta, start_ref, q_ref, k_ref, v_ref, go_ref, o_ref, lse_ref,
    dq_ref, dkv_ref, bias_ref, q_rows, go_rows, dq_acc, delta_ref,
):
    rows = q_ref.shape[1]
    size = k_ref.shape[2]
    low, high, q_start, at_x = meta[0], meta[1], meta[2], meta[3]

    @pl.when(pl.program_id(0) == 0)
    def _():
        q_pos = q_start + lax.broadcasted_iota(jnp.int32, (size, rows), 1)
        subs = lax.broadcasted_iota(jnp.int32, (size, rows), 0)

        def fill(block, carry):
            key_pos = block * size + subs
            allowed = (key_pos >= start_ref[...]) & (key_pos <= q_pos)
            bias_ref[block] = jnp.where(allowed, 0.0, MASKED)
            return carry

        lax.fori_loop(low, high, fill, 0)

    q_cols = q_ref[...].T
    go_cols = go_ref[...].T
    for head in range(GROUP):
        part = slice(head * HEAD_DIM, (head + 1) * HEAD_DIM)
        q_rows[head] = q_cols[:, part]
        go_rows[head] = go_cols[:, part]
        delta_ref[head : head + 1, :] = jnp.sum(
            go_ref[part, :].astype(f32) * o_ref[part, :].astype(f32), axis=0, keepdims=True
        )
    dkv_ref[...] = jnp.zeros_like(dkv_ref)
    dq_acc[...] = jnp.zeros_like(dq_acc)

    def body(block, carry):
        slot = block_slot(block, at_x, xs)
        key_cols = k_ref[slot]
        key_rows = key_cols.T
        value_rows = v_ref[slot].T
        bias = bias_ref[block]
        dk = jnp.zeros((size, HEAD_DIM), f32)
        dv = jnp.zeros((size, HEAD_DIM), f32)
        for head in range(GROUP):
            part = slice(head * HEAD_DIM, (head + 1) * HEAD_DIM)
            raw = jnp.dot(key_rows, q_ref[part, :], preferred_element_type=f32)
            probs = jnp.exp2(
                raw * (SCORE_SCALE * LOG2E) + (bias - lse_ref[0, head : head + 1, :])
            )
            grad_probs = jnp.dot(value_rows, go_ref[part, :], preferred_element_type=f32)
            grad_scores = (probs * (grad_probs - delta_ref[head : head + 1, :])).astype(bf16)
            dv += jnp.dot(probs.astype(bf16), go_rows[head], preferred_element_type=f32)
            dk += jnp.dot(grad_scores, q_rows[head], preferred_element_type=f32)
            dq_acc[part, :] += jnp.dot(key_cols, grad_scores, preferred_element_type=f32)
        dkv_ref[slot, 0] = (SCORE_SCALE * dk).T.astype(bf16)
        dkv_ref[slot, 1] = dv.T.astype(bf16)
        return carry

    lax.fori_loop(low, high, body, 0)
    dq_ref[...] = (SCORE_SCALE * dq_acc[...]).astype(bf16)


def attend_forward(xs, meta, start_col, q_t, batch, window):
    rows = start_col.shape[0]
    blocks, _, size = window.shape
    wide = GROUP * HEAD_DIM
    return pl.pallas_call(
        functools.partial(forward_kernel, xs),
        name="attend_forward",
        grid_spec=pltpu.PrefetchScalarGridSpec(
            num_scalar_prefetch=1,
            grid=(KV_HEADS,),
            in_specs=[
                pl.BlockSpec((rows, 1), lambda g, m: (0, 0)),
                pl.BlockSpec((wide, rows), lambda g, m: (g, batch)),
                pl.BlockSpec((blocks, HEAD_DIM, size), lambda g, m: (0, g, 0)),
                pl.BlockSpec((blocks, HEAD_DIM, size), lambda g, m: (0, KV_HEADS + g, 0)),
            ],
            out_specs=[
                pl.BlockSpec((wide, rows), lambda g, m: (g, 0)),
                pl.BlockSpec((1, GROUP, rows), lambda g, m: (g, 0, 0)),
            ],
            scratch_shapes=[
                pltpu.VMEM((blocks, rows, size), f32),
                pltpu.VMEM((GROUP, rows, HEAD_DIM), bf16),
                pltpu.VMEM((GROUP, rows, 2 * HEAD_DIM), f32),
            ],
        ),
        out_shape=[
            jax.ShapeDtypeStruct((Q_WIDTH, rows), bf16),
            jax.ShapeDtypeStruct((KV_HEADS, GROUP, rows), f32),
        ],
        cost_estimate=pl.CostEstimate(
            flops=4 * HEADS * rows * blocks * size * 128, bytes_accessed=4 * 1024 * 1024,
            transcendentals=HEADS * rows * blocks * size,
        ),
    )(meta, start_col, q_t, window, window)


def attend_backward(xs, meta, start_row, q_t, batch, window, go_t, o_t, lse):
    rows = start_row.shape[1]
    blocks, _, size = window.shape
    wide = GROUP * HEAD_DIM
    return pl.pallas_call(
        functools.partial(backward_kernel, xs),
        name="attend_backward",
        grid_spec=pltpu.PrefetchScalarGridSpec(
            num_scalar_prefetch=1,
            grid=(KV_HEADS,),
            in_specs=[
                pl.BlockSpec((1, rows), lambda g, m: (0, 0)),
                pl.BlockSpec((wide, rows), lambda g, m: (g, batch)),
                pl.BlockSpec((blocks, HEAD_DIM, size), lambda g, m: (0, g, 0)),
                pl.BlockSpec((blocks, HEAD_DIM, size), lambda g, m: (0, KV_HEADS + g, 0)),
                pl.BlockSpec((wide, rows), lambda g, m: (g, 0)),
                pl.BlockSpec((wide, rows), lambda g, m: (g, 0)),
                pl.BlockSpec((1, GROUP, rows), lambda g, m: (g, 0, 0)),
            ],
            out_specs=[
                pl.BlockSpec((wide, rows), lambda g, m: (g, 0)),
                pl.BlockSpec((blocks, 2, HEAD_DIM, size), lambda g, m: (0, 0, g, 0)),
            ],
            scratch_shapes=[
                pltpu.VMEM((blocks, size, rows), f32),
                pltpu.VMEM((GROUP, rows, HEAD_DIM), bf16),
                pltpu.VMEM((GROUP, rows, HEAD_DIM), bf16),
                pltpu.VMEM((wide, rows), f32),
                pltpu.VMEM((8, rows), f32),
            ],
        ),
        out_shape=[
            jax.ShapeDtypeStruct((Q_WIDTH, rows), bf16),
            jax.ShapeDtypeStruct((blocks, 2, KV_WIDTH, size), bf16),
        ],
        cost_estimate=pl.CostEstimate(
            flops=10 * HEADS * rows * blocks * size * 128, bytes_accessed=8 * 1024 * 1024,
            transcendentals=HEADS * rows * blocks * size,
        ),
    )(meta, start_row, q_t, window, window, go_t, o_t, lse)


LAYOUT = "yczx"
CTX = ("z", "x")
DOC_ROWS = 16


def after(value, *earlier):
    return lax.optimization_barrier((value, *earlier))[0]


class Transfers:
    def __init__(self, sizes):
        self.sizes = sizes

    def shift(self, value, axis, step):
        size = self.sizes[axis]
        return lax.ppermute(value, axis, [(i, (i + step) % size) for i in range(size)])

    def hop(self, value, axis, step):
        size = self.sizes[axis]
        pairs = [(i, i + step) for i in range(size) if 0 <= i + step < size]
        return lax.ppermute(value, axis, pairs)

    def place(self, pieces, axis, dim):
        size = self.sizes[axis]
        if size == 1:
            return jnp.expand_dims(pieces[0], dim)
        shape = pieces[0].shape
        rank = len(shape) + 1
        index = lax.broadcasted_iota(
            jnp.int32, tuple(size if d == dim else 1 for d in range(rank)), dim
        )
        back = jnp.mod(lax.axis_index(axis) - index, size)
        whole = jnp.broadcast_to(
            jnp.expand_dims(pieces[0], dim), shape[:dim] + (size,) + shape[dim:]
        )
        for k in range(1, size):
            whole = jnp.where(back == k, jnp.expand_dims(pieces[k], dim), whole)
        return whole

    def ring(self, value, axis):
        pieces = [value]
        for _ in range(1, self.sizes[axis]):
            pieces.append(self.shift(pieces[-1], axis, 1))
        return pieces

    def direct(self, value, axis):
        return [value] + [self.shift(value, axis, k) for k in range(1, self.sizes[axis])]

    def total(self, value, axis):
        size, step = self.sizes[axis], 1
        while step < size:
            value = value + lax.ppermute(value, axis, [(i, i ^ step) for i in range(size)])
            step *= 2
        return value

    def gather(self, value, axis, dim):
        return self.place(self.ring(value, axis), axis, dim)

    def take(self, value, axis, dim, step):
        size = self.sizes[axis]
        index = jnp.mod(lax.axis_index(axis) + step, size)
        return lax.dynamic_index_in_dim(value, index, dim, keepdims=False)

    def scatter(self, value, axis, dim):
        total = self.take(value, axis, dim, 0).astype(f32)
        for k in range(1, self.sizes[axis]):
            sent = self.take(value, axis, dim, k).astype(bf16)
            total = total + self.shift(sent, axis, k).astype(f32)
        return total

    def exchange(self, value, axis, dim, out_dim):
        pieces = [self.take(value, axis, dim, 0)]
        for k in range(1, self.sizes[axis]):
            pieces.append(self.shift(self.take(value, axis, dim, k), axis, k))
        return self.place(pieces, axis, out_dim)

    def spread(self, pieces, order):
        value = self.place(pieces, "z", 0)
        have = ["z"]
        for axis in order:
            dim = sum(1 for a in have if LAYOUT.index(a) < LAYOUT.index(axis))
            value = self.gather(value, axis, dim)
            have.append(axis)
        return value

    def scatter_chips(self, value, order):
        have = [axis for axis in LAYOUT if axis in order]
        for number, axis in enumerate(order):
            value = self.scatter(value, axis, have.index(axis))
            if number < len(order) - 1:
                value = value.astype(bf16)
            have.remove(axis)
        return value


def head_forward(lin, gain, cosine, sine):
    scale = lax.rsqrt(jnp.mean(lin * lin, axis=1, keepdims=True) + EPS)
    normal = lin * scale * gain[None, :, None]
    half = HEAD_DIM // 2
    first, second = normal[:, :half], normal[:, half:]
    turned = jnp.concatenate(
        [first * cosine - second * sine, second * cosine + first * sine], axis=1
    )
    return turned, scale


def head_backward(grad, lin, scale, gain, cosine, sine):
    half = HEAD_DIM // 2
    first, second = grad[:, :half], grad[:, half:]
    back = jnp.concatenate(
        [first * cosine + second * sine, second * cosine - first * sine], axis=1
    )
    gain_grad = jnp.sum(back * lin * scale, axis=(0, 2))
    scaled = back * gain[None, :, None]
    lin_grad = scale * scaled - lin * (scale**3) * jnp.mean(scaled * lin, axis=1, keepdims=True)
    return lin_grad, gain_grad


def row_scale(values):
    return lax.rsqrt(jnp.mean(values * values, axis=-1, keepdims=True) + EPS)


def norm_backward(grad, values, scale):
    return scale * grad - values * (scale**3) * jnp.mean(grad * values, axis=-1, keepdims=True)


def per_device(
    sizes, tokens, out_grad, doc_ids, corpus, corpus_weight, attn_gain, w_query, w_key, w_value,
    query_gain, key_gain, w_out, ffn_gain, w_gate, w_up, w_down,
):
    move = Transfers(sizes)
    ys, cs, zs, xs = (sizes[a] for a in LAYOUT)
    batches, local, width = tokens.shape
    both_rows = batches * local
    span = xs * local
    back_groups = -(-(DOC_MOST - 1) // span)
    at_z, at_x = lax.axis_index("z"), lax.axis_index("x")
    ffn_part = w_gate.shape[1] // (ys * cs)
    d_rows = w_gate.shape[0]
    parts = [slice(b * local, (b + 1) * local) for b in range(batches)]

    gain_a = attn_gain.astype(f32)[:, None]
    gain_f = ffn_gain.astype(f32)[:, None]
    w_kv = jnp.concatenate([w_key, w_value], axis=1)
    kv_near = move.direct((w_kv.astype(f32) * gain_a).astype(bf16), "z")
    w_q_low = (w_query.astype(f32) * gain_a).astype(bf16)
    q_near = move.direct(w_q_low, "z")
    w_kv_all = move.spread(kv_near, "xyc").reshape(width, 2 * KV_WIDTH)
    w_q_all = move.spread(q_near, "xyc").reshape(width, Q_WIDTH)
    w_out_all = lax.all_gather(w_out, tuple(LAYOUT), axis=0, tiled=True)

    w_gate_low = (w_gate.astype(f32) * gain_f).astype(bf16).reshape(d_rows, ys, cs, 1, ffn_part)
    w_up_low = (w_up.astype(f32) * gain_f).astype(bf16).reshape(d_rows, ys, cs, 1, ffn_part)
    both = jnp.concatenate([w_gate_low, w_up_low], axis=3).reshape(d_rows, ys, cs, 2 * ffn_part)
    both = move.exchange(both, "c", 2, 0)
    both = move.exchange(both, "y", 2, 0)
    both = lax.all_gather(both, CTX, axis=0)
    w_down_all = lax.all_gather(w_down, CTX, axis=0, tiled=True)
    w_both = both.transpose(1, 2, 0, 3, 4).reshape(width, 2 * ffn_part)

    q_start = back_groups * span + at_x * local
    high = back_groups * xs + at_x + 1

    half_dim = HEAD_DIM // 2
    frequency = jnp.exp(
        jnp.arange(half_dim, dtype=f32) * (-2.0 * math.log(10000.0) / HEAD_DIM)
    )
    positions = (at_z * xs + at_x) * local + jnp.arange(local, dtype=jnp.int32)
    angles = frequency[:, None] * jnp.tile(positions, batches).astype(f32)[None, :]
    cosine, sine = jnp.cos(angles)[None], jnp.sin(angles)[None]
    gain_q, gain_k = query_gain.astype(f32), key_gain.astype(f32)

    tag_range = jnp.arange(TAGS, dtype=jnp.int32)
    grads_out = [
        jnp.sum(jnp.where(tag_range == corpus[b], corpus_weight, 0.0)) * out_grad[b].astype(f32)
        for b in range(batches)
    ]

    def seq_blocks(rows):
        chips = move.ring(rows, "y")
        blocks = list(chips)
        for k in range(1, cs):
            blocks += [move.shift(chip, "c", k) for chip in chips]
        return blocks

    def seq_gather(rows):
        return jnp.concatenate(seq_blocks(rows), axis=0)

    def core_sum(partial):
        blocks = partial.reshape(cs, ys, local, width)
        total = blocks[0].astype(f32)
        for k in range(1, cs):
            total = total + move.shift(blocks[k], "c", -k).astype(f32)
        return [total[0]] + [total[k].astype(bf16) for k in range(1, ys)]

    def chip_sum(rows):
        result = rows[0]
        for k in range(1, ys):
            result = result + move.shift(rows[k], "y", -k).astype(f32)
        return result

    grad_blocks = seq_blocks(
        after(jnp.concatenate(grads_out, axis=0).astype(bf16), w_q_all)
    )
    grads_all = [jnp.concatenate([g[part] for g in grad_blocks], axis=0) for part in parts]

    inputs = after(tokens, *kv_near[1:]).reshape(both_rows, width).astype(f32)
    scale_in = row_scale(inputs)
    normed = (inputs * scale_in).astype(bf16)
    kv_lin = dot(w_kv_all, normed, 0, 1)
    key_lin = kv_lin[:KV_WIDTH].reshape(KV_HEADS, HEAD_DIM, both_rows)
    key_rot, key_scale = head_forward(key_lin, gain_k, cosine, sine)
    kv = jnp.concatenate(
        [
            key_rot.astype(bf16).reshape(KV_WIDTH, both_rows),
            kv_lin[KV_WIDTH:].astype(bf16),
            jnp.broadcast_to(doc_ids.reshape(1, both_rows).astype(bf16), (DOC_ROWS, both_rows)),
        ],
        axis=0,
    )
    hops = [kv]
    for _ in range(back_groups):
        hops.append(move.hop(hops[-1], "z", 1))
    blocks = []
    for group in hops[::-1]:
        blocks += move.direct(group, "x")
    windows = [jnp.stack([block[:, part] for block in blocks]) for part in parts]
    present = at_z + jnp.repeat(jnp.arange(back_groups + 1), xs) >= back_groups
    starts = []
    for b in range(batches):
        docs = jnp.where(present[:, None], windows[b][:, 2 * KV_WIDTH].astype(jnp.int32), -1)
        below = docs.reshape(1, -1) < doc_ids[b][:, None]
        starts.append(jnp.sum(below.astype(jnp.int32), axis=1))

    half = Q_WIDTH // 2
    query_lin = jnp.concatenate(
        [dot(w_q_all[:, :half], normed, 0, 1), dot(w_q_all[:, half:], normed, 0, 1)], axis=0
    ).reshape(HEADS, HEAD_DIM, both_rows)
    query_rot, query_scale = head_forward(query_lin, gain_q, cosine, sine)
    query_t = query_rot.astype(bf16).reshape(Q_WIDTH, both_rows)

    metas, mixed, lses, resids, scale_mids, normed2_all = [], [], [], [], [], []
    for b, part in enumerate(parts):
        meta = jnp.stack([starts[b][0] // local, high, q_start, at_x]).astype(jnp.int32)
        mixed_t, lse = attend_forward(xs, meta, starts[b][:, None], query_t, b, windows[b])
        resid = inputs[part] + dot(mixed_t, w_out_all, 0, 0)
        scale_mid = row_scale(resid)
        normed2_all.append(seq_gather((resid * scale_mid).astype(bf16)))
        metas.append(meta)
        mixed.append(mixed_t)
        lses.append(lse)
        resids.append(resid)
        scale_mids.append(scale_mid)

    hiddens, gate_grads, up_grads, sums = [], [], [], []
    for b in range(batches):
        wide = matmul(normed2_all[b], w_both)
        gate, up = wide[:, :ffn_part], wide[:, ffn_part:]
        sig = jax.nn.sigmoid(gate)
        silu = gate * sig
        hiddens.append((silu * up).astype(bf16))
        grads = after(grads_all[b], *sums[-1][1:]) if sums else grads_all[b]
        grad_hidden = dot(grads, w_down_all, 1, 1)
        grad_gate = (grad_hidden * up * (sig * (1.0 + gate * (1.0 - sig)))).astype(bf16)
        grad_up = (grad_hidden * silu).astype(bf16)
        grad_wide = jnp.concatenate([grad_gate, grad_up], axis=1)
        sums.append(core_sum(dot(grad_wide, w_both, 1, 1).astype(bf16)))
        gate_grads.append(grad_gate)
        up_grads.append(grad_up)

    grad_resids, low_grads = [], []
    for b in range(batches):
        grad_normed2 = chip_sum(sums[b])
        grad_resid = grads_out[b] + norm_backward(grad_normed2, resids[b], scale_mids[b])
        grad_resids.append(grad_resid)
        low_grads.append(grad_resid.astype(bf16))

    def token_sum(lefts, rights):
        total = dot(lefts[0], rights[0], 0, 0)
        for left, right in zip(lefts[1:], rights[1:]):
            total = total + dot(left, right, 0, 0)
        return total.astype(bf16)

    def scatter_columns(lefts, rights):
        value = token_sum(lefts, rights).reshape(ys * cs, zs * xs * d_rows, ffn_part)
        return lax.psum_scatter(value, CTX, scatter_dimension=1, tiled=True)

    gate_sum = scatter_columns(normed2_all, gate_grads)
    up_sum = scatter_columns(normed2_all, [after(g, *sums[-1][1:]) for g in up_grads])
    late = after(hiddens[0], *sums[-1][1:])
    grad_down = lax.psum_scatter(
        token_sum([late] + hiddens[1:], grads_all), CTX, scatter_dimension=0, tiled=True
    ).astype(f32)

    query_grads, groups = [], []
    for b in range(batches):
        grad_mixed_t = dot(w_out_all, low_grads[b], 1, 1).astype(bf16)
        dq_t, dkv = attend_backward(
            xs, metas[b], starts[b][None, :], query_t, b, windows[b], grad_mixed_t, mixed[b],
            lses[b],
        )
        query_grads.append(dq_t)
        groups.append(dkv.reshape(back_groups + 1, xs, 2 * KV_WIDTH, local))

    def split_cores(value, rows):
        value = value.astype(bf16).reshape(ys, cs, zs, xs, rows, -1)
        return move.scatter(value, "c", 1).astype(bf16)

    out_cores = split_cores(
        matmul(jnp.concatenate(mixed, axis=1), jnp.concatenate(low_grads, axis=0)),
        w_out.shape[0],
    )
    query_grad, gq_gain = head_backward(
        jnp.concatenate(query_grads, axis=1).astype(f32).reshape(HEADS, HEAD_DIM, both_rows),
        query_lin, query_scale, gain_q, cosine, sine,
    )
    query_grad = query_grad.astype(bf16).reshape(Q_WIDTH, both_rows)
    q_cores = split_cores(dot(normed, query_grad, 0, 1), d_rows)

    kv_grads = []
    for b in range(batches):
        carried = groups[b][0]
        for k in range(1, back_groups + 1):
            if b == batches - 1 and k == back_groups:
                carried = after(carried, out_cores, q_cores)
            carried = (
                move.hop(carried, "z", -1).astype(f32) + groups[b][k].astype(f32)
            ).astype(bf16)
        total = carried[0].astype(f32)
        for k in range(1, xs):
            total = total + move.shift(carried[k], "x", -k).astype(f32)
        kv_grads.append(total)
    grad_out_w = move.scatter_chips(out_cores, "yxz")
    grad_q_w = move.scatter_chips(q_cores, "xyz")

    kv_sum = jnp.concatenate(kv_grads, axis=1)
    key_grad, gk_gain = head_backward(
        kv_sum[:KV_WIDTH].reshape(KV_HEADS, HEAD_DIM, both_rows), key_lin, key_scale, gain_k,
        cosine, sine,
    )
    kv_grad = jnp.concatenate(
        [key_grad.astype(bf16).reshape(KV_WIDTH, both_rows), kv_sum[KV_WIDTH:].astype(bf16)],
        axis=0,
    )
    grad_kv_w = move.scatter_chips(split_cores(dot(normed, kv_grad, 0, 1), d_rows), "yxz")
    grad_normed = dot(query_grad, w_q_all, 0, 1) + dot(kv_grad, w_kv_all, 0, 1)
    normed_back = norm_backward(grad_normed, inputs, scale_in)
    token_grads = [
        (grad_resids[b] + normed_back[part]).astype(bf16) for b, part in enumerate(parts)
    ]

    outputs = []
    for b in range(batches):
        hidden = after(hiddens[b], low_grads[-1])
        rows = core_sum(matmul(hidden, w_down_all).astype(bf16))
        outputs.append((resids[b] + chip_sum(rows)).astype(bf16))

    both_sum = jnp.concatenate([gate_sum, up_sum], axis=2).reshape(ys, cs, d_rows, -1)
    both_sum = move.exchange(both_sum, "y", 0, 2)
    both_sum = move.exchange(both_sum, "c", 0, 2).astype(f32)
    grad_gate_w = both_sum[..., :ffn_part].reshape(d_rows, -1)
    grad_up_w = both_sum[..., ffn_part:].reshape(d_rows, -1)

    attn_gain_grad = jnp.sum(grad_q_w * w_query.astype(f32), axis=1) + jnp.sum(
        grad_kv_w * w_kv.astype(f32), axis=1
    )
    ffn_gain_grad = jnp.sum(
        grad_gate_w * w_gate.astype(f32) + grad_up_w * w_up.astype(f32), axis=1
    )
    grad_kv_w = grad_kv_w * gain_a
    small = jnp.concatenate([gq_gain, gk_gain])[None, :]
    for axis in LAYOUT:
        small = move.total(small, axis)

    return (
        jnp.stack(outputs),
        jnp.stack(token_grads),
        attn_gain_grad,
        grad_q_w * gain_a,
        grad_kv_w[:, :KV_WIDTH],
        grad_kv_w[:, KV_WIDTH:],
        small[0, :HEAD_DIM],
        small[0, HEAD_DIM:],
        grad_out_w,
        ffn_gain_grad,
        grad_gate_w * gain_f,
        grad_up_w * gain_f,
        grad_down,
    )


def solution(mesh):
    sizes = {"c": 2, "z": Z_CHIPS}
    sizes["y"] = mesh.shape["seq"] // sizes["c"]
    sizes["x"] = mesh.shape["ctx"] // sizes["z"]
    grid = Mesh(mesh.devices.reshape([sizes[a] for a in "yczx"]), ("y", "c", "z", "x"))
    seq, ctx, every = ("y", "c"), ("z", "x"), ("y", "c", "z", "x")
    acts, vector, matrix = P(seq, ctx, None), P(every), P(every, None)
    in_specs = (
        acts, acts, P(seq, ctx), P(seq), P(), vector, matrix, matrix, matrix, P(), P(), matrix,
        vector, matrix, matrix, matrix,
    )
    out_specs = (
        acts, acts, vector, matrix, matrix, matrix, P(), P(), matrix, vector, matrix, matrix,
        matrix,
    )
    return jax.shard_map(
        functools.partial(per_device, sizes), mesh=grid, in_specs=in_specs, out_specs=out_specs,
        check_vma=False,
    )
```

```python
import functools
import math

import jax
import jax.numpy as jnp
import numpy as np
from jax import lax
from jax.experimental import pallas as pl
from jax.experimental.pallas import tpu as pltpu
from jax.sharding import Mesh
from jax.sharding import PartitionSpec as P

HEADS = 20
KV_HEADS = 5
GROUP = HEADS // KV_HEADS
HEAD_DIM = 64
TAGS = 4
Q_WIDTH = HEADS * HEAD_DIM
KV_WIDTH = KV_HEADS * HEAD_DIM
DOC_MOST = 1024
Z_CHIPS = 4
EPS = 1e-06
SCORE_SCALE = 0.125
LOG2E = math.log2(math.e)
MASKED = -1e30

FLAGS = {'wo': 0, 'ybo': 2, 'qg': 0, 'og': 1, 'xq': 0, 'att1': 1, 'ogc': 0, 'gh1': 1, 'dn': 4, 'ou': 5, 'h0': 0, 'ga': 1, 'wg': 0, 'h1': 0, 'up': 1, 's': 0, 'hc': 1, 't': 0, 'oa': 'y', 'qa': 'x', 'w1': 3, 'tl': 3, 'sm': 1, 'bs': 1}
bf16 = jnp.bfloat16
f32 = jnp.float32


def dot(left, right, left_dim, right_dim):
    return lax.dot_general(
        left, right, (((left_dim,), (right_dim,)), ((), ())), preferred_element_type=f32
    )


def matmul(left, right):
    return dot(left, right, 1, 0)


def block_slot(block, at_x, xs):
    return (block // xs) * xs + lax.rem(at_x - lax.rem(block, xs) + xs, xs)


def forward_kernel(xs, meta, start_ref, q_ref, k_ref, v_ref, o_ref, lse_ref, bias_ref, q_rows, acc):
    rows = q_ref.shape[1]
    size = k_ref.shape[2]
    low, high, q_start, at_x = meta[0], meta[1], meta[2], meta[3]

    @pl.when(pl.program_id(0) == 0)
    def _():
        q_pos = q_start + lax.broadcasted_iota(jnp.int32, (rows, size), 0)
        lanes = lax.broadcasted_iota(jnp.int32, (rows, size), 1)

        def fill(block, carry):
            key_pos = block * size + lanes
            allowed = (key_pos >= start_ref[...]) & (key_pos <= q_pos)
            bias_ref[block] = jnp.where(allowed, 0.0, MASKED)
            return carry

        lax.fori_loop(low, high, fill, 0)

    q_cols = q_ref[...].T
    for head in range(GROUP):
        q_rows[head] = q_cols[:, head * HEAD_DIM : (head + 1) * HEAD_DIM]
    sub = lax.broadcasted_iota(jnp.int32, (HEAD_DIM, size), 0)
    ones = jnp.where(sub == 0, 1.0, 0.0).astype(bf16)
    acc[...] = jnp.zeros_like(acc)

    def body(block, carry):
        slot = block_slot(block, at_x, xs)
        key_cols = k_ref[slot]
        value_rows = jnp.concatenate([v_ref[slot], ones], axis=0).T
        bias = bias_ref[block]
        for head in range(GROUP):
            raw = jnp.dot(q_rows[head], key_cols, preferred_element_type=f32)
            probs = jnp.exp2(raw * (SCORE_SCALE * LOG2E) + bias).astype(bf16)
            acc[head] += jnp.dot(probs, value_rows, preferred_element_type=f32)
        return carry

    lax.fori_loop(low, high, body, 0)
    for head in range(GROUP):
        turned = acc[head].T
        total = turned[HEAD_DIM : HEAD_DIM + 1, :]
        o_ref[head * HEAD_DIM : (head + 1) * HEAD_DIM, :] = (turned[:HEAD_DIM] / total).astype(bf16)
        lse_ref[0, head : head + 1, :] = jnp.log2(total)


def backward_kernel(
    xs, meta, start_ref, q_ref, k_ref, v_ref, go_ref, o_ref, lse_ref,
    dq_ref, dkv_ref, bias_ref, q_rows, go_rows, dq_acc, delta_ref,
):
    rows = q_ref.shape[1]
    size = k_ref.shape[2]
    low, high, q_start, at_x = meta[0], meta[1], meta[2], meta[3]

    @pl.when(pl.program_id(0) == 0)
    def _():
        q_pos = q_start + lax.broadcasted_iota(jnp.int32, (size, rows), 1)
        subs = lax.broadcasted_iota(jnp.int32, (size, rows), 0)

        def fill(block, carry):
            key_pos = block * size + subs
            allowed = (key_pos >= start_ref[...]) & (key_pos <= q_pos)
            bias_ref[block] = jnp.where(allowed, 0.0, MASKED)
            return carry

        lax.fori_loop(low, high, fill, 0)

    q_cols = q_ref[...].T
    go_cols = go_ref[...].T
    for head in range(GROUP):
        part = slice(head * HEAD_DIM, (head + 1) * HEAD_DIM)
        q_rows[head] = q_cols[:, part]
        go_rows[head] = go_cols[:, part]
        delta_ref[head : head + 1, :] = jnp.sum(
            go_ref[part, :].astype(f32) * o_ref[part, :].astype(f32), axis=0, keepdims=True
        )
    dkv_ref[...] = jnp.zeros_like(dkv_ref)
    dq_acc[...] = jnp.zeros_like(dq_acc)

    def body(block, carry):
        slot = block_slot(block, at_x, xs)
        key_cols = k_ref[slot]
        key_rows = key_cols.T
        value_rows = v_ref[slot].T
        bias = bias_ref[block]
        dk = jnp.zeros((size, HEAD_DIM), f32)
        dv = jnp.zeros((size, HEAD_DIM), f32)
        for head in range(GROUP):
            part = slice(head * HEAD_DIM, (head + 1) * HEAD_DIM)
            raw = jnp.dot(key_rows, q_ref[part, :], preferred_element_type=f32)
            probs = jnp.exp2(
                raw * (SCORE_SCALE * LOG2E) + (bias - lse_ref[0, head : head + 1, :])
            )
            grad_probs = jnp.dot(value_rows, go_ref[part, :], preferred_element_type=f32)
            grad_scores = (probs * (grad_probs - delta_ref[head : head + 1, :])).astype(bf16)
            dv += jnp.dot(probs.astype(bf16), go_rows[head], preferred_element_type=f32)
            dk += jnp.dot(grad_scores, q_rows[head], preferred_element_type=f32)
            dq_acc[part, :] += jnp.dot(key_cols, grad_scores, preferred_element_type=f32)
        dkv_ref[slot, 0] = (SCORE_SCALE * dk).T.astype(bf16)
        dkv_ref[slot, 1] = dv.T.astype(bf16)
        return carry

    lax.fori_loop(low, high, body, 0)
    dq_ref[...] = (SCORE_SCALE * dq_acc[...]).astype(bf16)


def attend_forward(xs, meta, start_col, q_t, batch, window):
    rows = start_col.shape[0]
    blocks, _, size = window.shape
    wide = GROUP * HEAD_DIM
    return pl.pallas_call(
        functools.partial(forward_kernel, xs),
        name="attend_forward",
        grid_spec=pltpu.PrefetchScalarGridSpec(
            num_scalar_prefetch=1,
            grid=(KV_HEADS,),
            in_specs=[
                pl.BlockSpec((rows, 1), lambda g, m: (0, 0)),
                pl.BlockSpec((wide, rows), lambda g, m: (g, batch)),
                pl.BlockSpec((blocks, HEAD_DIM, size), lambda g, m: (0, g, 0)),
                pl.BlockSpec((blocks, HEAD_DIM, size), lambda g, m: (0, KV_HEADS + g, 0)),
            ],
            out_specs=[
                pl.BlockSpec((wide, rows), lambda g, m: (g, 0)),
                pl.BlockSpec((1, GROUP, rows), lambda g, m: (g, 0, 0)),
            ],
            scratch_shapes=[
                pltpu.VMEM((blocks, rows, size), f32),
                pltpu.VMEM((GROUP, rows, HEAD_DIM), bf16),
                pltpu.VMEM((GROUP, rows, 2 * HEAD_DIM), f32),
            ],
        ),
        out_shape=[
            jax.ShapeDtypeStruct((Q_WIDTH, rows), bf16),
            jax.ShapeDtypeStruct((KV_HEADS, GROUP, rows), f32),
        ],
        cost_estimate=pl.CostEstimate(
            flops=4 * HEADS * rows * blocks * size * 128, bytes_accessed=4 * 1024 * 1024,
            transcendentals=HEADS * rows * blocks * size,
        ),
    )(meta, start_col, q_t, window, window)


def attend_backward(xs, meta, start_row, q_t, batch, window, go_t, o_t, lse):
    rows = start_row.shape[1]
    blocks, _, size = window.shape
    wide = GROUP * HEAD_DIM
    return pl.pallas_call(
        functools.partial(backward_kernel, xs),
        name="attend_backward",
        grid_spec=pltpu.PrefetchScalarGridSpec(
            num_scalar_prefetch=1,
            grid=(KV_HEADS,),
            in_specs=[
                pl.BlockSpec((1, rows), lambda g, m: (0, 0)),
                pl.BlockSpec((wide, rows), lambda g, m: (g, batch)),
                pl.BlockSpec((blocks, HEAD_DIM, size), lambda g, m: (0, g, 0)),
                pl.BlockSpec((blocks, HEAD_DIM, size), lambda g, m: (0, KV_HEADS + g, 0)),
                pl.BlockSpec((wide, rows), lambda g, m: (g, 0)),
                pl.BlockSpec((wide, rows), lambda g, m: (g, 0)),
                pl.BlockSpec((1, GROUP, rows), lambda g, m: (g, 0, 0)),
            ],
            out_specs=[
                pl.BlockSpec((wide, rows), lambda g, m: (g, 0)),
                pl.BlockSpec((blocks, 2, HEAD_DIM, size), lambda g, m: (0, 0, g, 0)),
            ],
            scratch_shapes=[
                pltpu.VMEM((blocks, size, rows), f32),
                pltpu.VMEM((GROUP, rows, HEAD_DIM), bf16),
                pltpu.VMEM((GROUP, rows, HEAD_DIM), bf16),
                pltpu.VMEM((wide, rows), f32),
                pltpu.VMEM((8, rows), f32),
            ],
        ),
        out_shape=[
            jax.ShapeDtypeStruct((Q_WIDTH, rows), bf16),
            jax.ShapeDtypeStruct((blocks, 2, KV_WIDTH, size), bf16),
        ],
        cost_estimate=pl.CostEstimate(
            flops=10 * HEADS * rows * blocks * size * 128, bytes_accessed=8 * 1024 * 1024,
            transcendentals=HEADS * rows * blocks * size,
        ),
    )(meta, start_row, q_t, window, window, go_t, o_t, lse)


LAYOUT = "yczx"
CTX = ("z", "x")
DOC_ROWS = 16


def opt(name, default=0):
    return FLAGS.get(name, default)


def after(value, *earlier):
    return lax.optimization_barrier((value, *earlier))[0] if earlier else value


class Transfers:
    def __init__(self, sizes):
        self.sizes = sizes

    def shift(self, value, axis, step):
        size = self.sizes[axis]
        return lax.ppermute(value, axis, [(i, (i + step) % size) for i in range(size)])

    def hop(self, value, axis, step):
        size = self.sizes[axis]
        pairs = [(i, i + step) for i in range(size) if 0 <= i + step < size]
        return lax.ppermute(value, axis, pairs)

    def place(self, pieces, axis, dim):
        size = self.sizes[axis]
        if size == 1:
            return jnp.expand_dims(pieces[0], dim)
        shape = pieces[0].shape
        rank = len(shape) + 1
        index = lax.broadcasted_iota(
            jnp.int32, tuple(size if d == dim else 1 for d in range(rank)), dim
        )
        back = jnp.mod(lax.axis_index(axis) - index, size)
        whole = jnp.broadcast_to(
            jnp.expand_dims(pieces[0], dim), shape[:dim] + (size,) + shape[dim:]
        )
        for k in range(1, size):
            whole = jnp.where(back == k, jnp.expand_dims(pieces[k], dim), whole)
        return whole

    def ring(self, value, axis):
        pieces = [value]
        for _ in range(1, self.sizes[axis]):
            pieces.append(self.shift(pieces[-1], axis, 1))
        return pieces

    def direct(self, value, axis):
        return [value] + [self.shift(value, axis, k) for k in range(1, self.sizes[axis])]

    def total(self, value, axis):
        size, step = self.sizes[axis], 1
        while step < size:
            value = value + lax.ppermute(value, axis, [(i, i ^ step) for i in range(size)])
            step *= 2
        return value

    def gather(self, value, axis, dim):
        return self.place(self.ring(value, axis), axis, dim)

    def take(self, value, axis, dim, step):
        size = self.sizes[axis]
        index = jnp.mod(lax.axis_index(axis) + step, size)
        return lax.dynamic_index_in_dim(value, index, dim, keepdims=False)

    def scatter(self, value, axis, dim):
        total = self.take(value, axis, dim, 0).astype(f32)
        for k in range(1, self.sizes[axis]):
            sent = self.take(value, axis, dim, k).astype(bf16)
            total = total + self.shift(sent, axis, k).astype(f32)
        return total

    def exchange(self, value, axis, dim, out_dim):
        pieces = [self.take(value, axis, dim, 0)]
        for k in range(1, self.sizes[axis]):
            pieces.append(self.shift(self.take(value, axis, dim, k), axis, k))
        return self.place(pieces, axis, out_dim)

    def spread(self, pieces, order, *earlier):
        value = self.place(pieces, "z", 0)
        have = ["z"]
        for axis in order:
            if earlier and axis == order[-1]:
                value = after(value, *earlier)
            dim = sum(1 for a in have if LAYOUT.index(a) < LAYOUT.index(axis))
            value = self.gather(value, axis, dim)
            have.append(axis)
        return value

    def scatter_chips(self, value, order):
        have = [axis for axis in LAYOUT if axis in order]
        for number, axis in enumerate(order):
            value = self.scatter(value, axis, have.index(axis))
            if number < len(order) - 1:
                value = value.astype(bf16)
            have.remove(axis)
        return value


def head_forward(lin, gain, cosine, sine):
    scale = lax.rsqrt(jnp.mean(lin * lin, axis=1, keepdims=True) + EPS)
    normal = lin * scale * gain[None, :, None]
    half = HEAD_DIM // 2
    first, second = normal[:, :half], normal[:, half:]
    turned = jnp.concatenate(
        [first * cosine - second * sine, second * cosine + first * sine], axis=1
    )
    return turned, scale


def head_backward(grad, lin, scale, gain, cosine, sine):
    half = HEAD_DIM // 2
    first, second = grad[:, :half], grad[:, half:]
    back = jnp.concatenate(
        [first * cosine + second * sine, second * cosine - first * sine], axis=1
    )
    gain_grad = jnp.sum(back * lin * scale, axis=(0, 2))
    scaled = back * gain[None, :, None]
    lin_grad = scale * scaled - lin * (scale**3) * jnp.mean(scaled * lin, axis=1, keepdims=True)
    return lin_grad, gain_grad


def row_scale(values):
    return lax.rsqrt(jnp.mean(values * values, axis=-1, keepdims=True) + EPS)


def norm_backward(grad, values, scale):
    return scale * grad - values * (scale**3) * jnp.mean(grad * values, axis=-1, keepdims=True)


def per_device(
    sizes, tokens, out_grad, doc_ids, corpus, corpus_weight, attn_gain, w_query, w_key, w_value,
    query_gain, key_gain, w_out, ffn_gain, w_gate, w_up, w_down,
):
    move = Transfers(sizes)
    ys, cs, zs, xs = (sizes[a] for a in LAYOUT)
    batches, local, width = tokens.shape
    both_rows = batches * local
    span = xs * local
    back_groups = -(-(DOC_MOST - 1) // span)
    at_z, at_x = lax.axis_index("z"), lax.axis_index("x")
    ffn_part = w_gate.shape[1] // (ys * cs)
    d_rows = w_gate.shape[0]
    parts = [slice(b * local, (b + 1) * local) for b in range(batches)]

    gain_a = attn_gain.astype(f32)[:, None]
    gain_f = ffn_gain.astype(f32)[:, None]
    w_kv = jnp.concatenate([w_key, w_value], axis=1)
    kv_near = move.direct((w_kv.astype(f32) * gain_a).astype(bf16), "z")
    w_q_low = (w_query.astype(f32) * gain_a).astype(bf16)
    q_near = move.direct(w_q_low, "z")
    kv_x = move.gather(move.place(kv_near, "z", 0), "x", 1)
    kv_xy = move.gather(kv_x, "y", 0)
    w_kv_all = move.gather(kv_xy, "c", 1).reshape(width, 2 * KV_WIDTH)
    if opt("wo"):
        out_near = move.direct(after(w_out, *(kv_near[1:] if opt("wo") == 1 else [])), "z")

    w_gate_low = (w_gate.astype(f32) * gain_f).astype(bf16).reshape(d_rows, ys, cs, 1, ffn_part)
    w_up_low = (w_up.astype(f32) * gain_f).astype(bf16).reshape(d_rows, ys, cs, 1, ffn_part)
    both = jnp.concatenate([w_gate_low, w_up_low], axis=3).reshape(d_rows, ys, cs, 2 * ffn_part)
    both = move.exchange(after(both, *(kv_near[:1] if opt("ybo") else [])), "c", 2, 0)
    both = move.exchange(after(both, *[[], kv_near[1:], [kv_x], [kv_xy]][opt("ybo")]), "y", 2, 0)
    both = lax.all_gather(both, CTX, axis=0)
    w_down_all = lax.all_gather(w_down, CTX, axis=0, tiled=True)
    w_both = both.transpose(1, 2, 0, 3, 4).reshape(width, 2 * ffn_part)

    q_start = back_groups * span + at_x * local
    high = back_groups * xs + at_x + 1

    half_dim = HEAD_DIM // 2
    frequency = jnp.exp(
        jnp.arange(half_dim, dtype=f32) * (-2.0 * math.log(10000.0) / HEAD_DIM)
    )
    positions = (at_z * xs + at_x) * local + jnp.arange(local, dtype=jnp.int32)
    angles = frequency[:, None] * jnp.tile(positions, batches).astype(f32)[None, :]
    cosine, sine = jnp.cos(angles)[None], jnp.sin(angles)[None]
    gain_q, gain_k = query_gain.astype(f32), key_gain.astype(f32)

    tag_range = jnp.arange(TAGS, dtype=jnp.int32)
    grads_out = [
        jnp.sum(jnp.where(tag_range == corpus[b], corpus_weight, 0.0)) * out_grad[b].astype(f32)
        for b in range(batches)
    ]

    def core_blocks(chips):
        blocks = list(chips)
        for k in range(1, cs):
            blocks += [move.shift(chip, "c", k) for chip in chips]
        return blocks

    def core_sum(partial):
        blocks = partial.reshape(cs, ys, local, width)
        total = blocks[0].astype(f32)
        for k in range(1, cs):
            total = total + move.shift(blocks[k], "c", -k).astype(f32)
        return [total[0]] + [total[k].astype(bf16) for k in range(1, ys)]

    def chip_sum(rows):
        result = rows[0]
        for k in range(1, ys):
            result = result + move.shift(rows[k], "y", -k).astype(f32)
        return result

    inputs = after(tokens, *kv_near[1:]).reshape(both_rows, width).astype(f32)
    scale_in = row_scale(inputs)
    normed = (inputs * scale_in).astype(bf16)
    kv_lin = dot(w_kv_all, normed, 0, 1)
    key_lin = kv_lin[:KV_WIDTH].reshape(KV_HEADS, HEAD_DIM, both_rows)
    key_rot, key_scale = head_forward(key_lin, gain_k, cosine, sine)
    kv = jnp.concatenate(
        [
            key_rot.astype(bf16).reshape(KV_WIDTH, both_rows),
            kv_lin[KV_WIDTH:].astype(bf16),
            jnp.broadcast_to(doc_ids.reshape(1, both_rows).astype(bf16), (DOC_ROWS, both_rows)),
        ],
        axis=0,
    )
    hops = [kv]
    for _ in range(back_groups):
        hops.append(move.hop(hops[-1], "z", 1))
    w_q_all = move.spread(q_near, opt("qord", "xyc"), *([kv] if opt("qg") else [])).reshape(width, Q_WIDTH)
    if opt("wo"):
        w_out_all = move.spread(
            out_near, opt("woord", "xyc"), *([hops[1]] if opt("wog") else [])
        ).reshape(Q_WIDTH, width)
    else:
        w_out_all = lax.all_gather(w_out, tuple(LAYOUT), axis=0, tiled=True)
    half = Q_WIDTH // 2
    query_lin = jnp.concatenate(
        [dot(w_q_all[:, :half], normed, 0, 1), dot(w_q_all[:, half:], normed, 0, 1)], axis=0
    ).reshape(HEADS, HEAD_DIM, both_rows)
    query_rot, query_scale = head_forward(query_lin, gain_q, cosine, sine)
    query_t = query_rot.astype(bf16).reshape(Q_WIDTH, both_rows)

    grad_chips = move.ring(
        after(
            jnp.concatenate(grads_out, axis=0).astype(bf16),
            *([[], [hops[1]], [kv], [w_q_all], [w_kv_all]][opt("og")]),
        ), "y"
    )

    blocks = []
    for number, group in enumerate(hops[::-1]):
        if number == 0 and opt("xq"):
            group = after(group, query_t)
        blocks += move.direct(group, "x")
    windows = [jnp.stack([block[:, part] for block in blocks]) for part in parts]
    present = at_z + jnp.repeat(jnp.arange(back_groups + 1), xs) >= back_groups
    starts = []
    for b in range(batches):
        docs = jnp.where(present[:, None], windows[b][:, 2 * KV_WIDTH].astype(jnp.int32), -1)
        below = docs.reshape(1, -1) < doc_ids[b][:, None]
        starts.append(jnp.sum(below.astype(jnp.int32), axis=1))

    if opt("eh") == 2:
        grad_blocks = core_blocks(grad_chips)
        grads_all = [jnp.concatenate([g[part] for g in grad_blocks], axis=0) for part in parts]
        early = [dot(g, w_down_all, 1, 1) for g in grads_all]
    metas, mixed, lses, resids, scale_mids, normed2_all = [], [], [], [], [], []
    rows, normed2_chips = None, []
    for b, part in enumerate(parts):
        meta = jnp.stack([starts[b][0] // local, high, q_start, at_x]).astype(jnp.int32)
        if rows is not None and opt("att1"):
            meta = after(meta, rows, *(early[:1] if opt("eh") == 2 else []))
        mixed_t, lse = attend_forward(xs, meta, starts[b][:, None], query_t, b, windows[b])
        resid = inputs[part] + dot(mixed_t, w_out_all, 0, 0)
        scale_mid = row_scale(resid)
        rows = (resid * scale_mid).astype(bf16)
        normed2_chips.append(move.ring(rows, "y"))
        metas.append(meta)
        mixed.append(mixed_t)
        lses.append(lse)
        resids.append(resid)
        scale_mids.append(scale_mid)

    grad_blocks = grad_blocks if opt("eh") == 2 else core_blocks(
        [after(chip, *([rows] if opt("ogc") else [])) for chip in grad_chips]
    )
    grads_all = [jnp.concatenate([g[part] for g in grad_blocks], axis=0) for part in parts]

    if opt("eh") == 1:
        early = [dot(g, w_down_all, 1, 1) for g in grads_all]
    hiddens, gate_grads, up_grads, sums = [], [], [], []
    for b in range(batches):
        chips = normed2_chips[b]
        if b > 0 and opt("w1"):
            chips = chips[:1] + [after(chip, [0, wide, grad_gate, partial][opt("w1")]) for chip in chips[1:]]
        normed2_all.append(jnp.concatenate(core_blocks(chips), axis=0))
        wide = matmul(normed2_all[b], w_both)
        gate, up = wide[:, :ffn_part], wide[:, ffn_part:]
        sig = jax.nn.sigmoid(gate)
        silu = gate * sig
        hiddens.append((silu * up).astype(bf16))
        grads = after(grads_all[b], *sums[-1][1:]) if sums and opt("gh1") else grads_all[b]
        grad_hidden = early[b] if opt("eh") else dot(grads, w_down_all, 1, 1)
        if sums and opt("eh") and opt("gh1"):
            grad_hidden = after(grad_hidden, *sums[-1][1:])
        grad_gate = (grad_hidden * up * (sig * (1.0 + gate * (1.0 - sig)))).astype(bf16)
        grad_up = (grad_hidden * silu).astype(bf16)
        grad_wide = jnp.concatenate([grad_gate, grad_up], axis=1)
        partial = dot(grad_wide, w_both, 1, 1).astype(bf16)
        sums.append(core_sum(partial))
        gate_grads.append(grad_gate)
        up_grads.append(grad_up)

    grad_resids, low_grads = [], []
    for b in range(batches):
        grad_normed2 = chip_sum(sums[b])
        grad_resid = grads_out[b] + norm_backward(grad_normed2, resids[b], scale_mids[b])
        grad_resids.append(grad_resid)
        low_grads.append(grad_resid.astype(bf16))

    def token_sum(lefts, rights):
        total = dot(lefts[0], rights[0], 0, 0)
        for left, right in zip(lefts[1:], rights[1:]):
            total = total + dot(left, right, 0, 0)
        return total.astype(bf16)

    def scatter_columns(total):
        value = total.reshape(ys * cs, zs * xs * d_rows, ffn_part)
        return lax.psum_scatter(value, CTX, scatter_dimension=1, tiled=True)

    late = [
        after(hidden, *[[], [partial], sums[-1][1:], [low_grads[0]]][opt("dn") % 4])
        for hidden in hiddens
    ]
    if opt("dn") < 4:
        down_total = token_sum(late, grads_all)
        grad_down = lax.psum_scatter(down_total, CTX, scatter_dimension=0, tiled=True).astype(f32)
    late = [
        after(hidden, *[[], [partial], sums[-1][1:], [low_grads[0]], low_grads][min(opt("ou"), 4)])
        for hidden in hiddens
    ]
    if opt("ou") < 5:
        out_rows = [core_sum(matmul(hidden, w_down_all).astype(bf16)) for hidden in late]

    def split_cores(value, rows):
        value = value.astype(bf16).reshape(ys, cs, zs, xs, rows, -1)
        return move.scatter(value, "c", 1).astype(bf16)

    query_grads, carried = [], []
    gate_total, held = None, []
    if opt("h0") & 1:
        held += [down_total]
    if opt("h0") & 2:
        held += [row for rows in out_rows for row in rows[1:]]
    for b in range(batches):
        low = after(low_grads[b], *held)
        grad_mixed_t = dot(w_out_all, low, 1, 1).astype(bf16)
        dq_t, dkv = attend_backward(
            xs, metas[b], starts[b][None, :], query_t, b, windows[b], grad_mixed_t, mixed[b],
            lses[b],
        )
        query_grads.append(dq_t)
        groups = dkv.reshape(back_groups + 1, xs, 2 * KV_WIDTH, local)
        first = (move.hop(groups[0], "z", -1).astype(f32) + groups[1].astype(f32)).astype(bf16)
        carried.append([first] + [groups[k] for k in range(2, back_groups + 1)])
        if gate_total is None:
            gate_total = token_sum(normed2_all, [after(gate_grads[0], *[[], [dq_t], sums[-1][1:], low_grads, [low_grads[0]] + sums[-1][1:]][opt("ga")])] + gate_grads[1:])
            out_cores = split_cores(
                matmul(
                    jnp.concatenate(mixed, axis=1),
                    jnp.concatenate([after(low_grads[0], *([dq_t] if opt("wg") else []))] + low_grads[1:], axis=0),
                ),
                w_out.shape[0],
            )
            held = []
            if opt("h1") & 1:
                held += [gate_total]
            if opt("h1") & 2:
                held += [out_cores]
            if opt("h1") & 4:
                held += [first]
    gate_sum = scatter_columns(gate_total)

    query_grad, gq_gain = head_backward(
        jnp.concatenate(query_grads, axis=1).astype(f32).reshape(HEADS, HEAD_DIM, both_rows),
        query_lin, query_scale, gain_q, cosine, sine,
    )
    query_grad = query_grad.astype(bf16).reshape(Q_WIDTH, both_rows)
    q_cores = split_cores(dot(normed, query_grad, 0, 1), d_rows)

    up_total = token_sum(normed2_all, [after(up_grads[0], *[[], [query_grads[0]], [query_grads[-1]], [carried[-1][0]], sums[-1][1:]][opt("up")])] + up_grads[1:])
    up_sum = scatter_columns(up_total)
    if opt("dn") >= 4:
        late = [after(hiddens[0], query_grads[opt("dn") - 4])] + hiddens[1:]
        down_total = token_sum(late, grads_all)
        grad_down = lax.psum_scatter(down_total, CTX, scatter_dimension=0, tiled=True).astype(f32)

    oa, qa = opt("oa", "x"), opt("qa", "y")
    out_chips = move.scatter(out_cores, oa, "yzx".index(oa)).astype(bf16)
    q_chips = move.scatter(q_cores, qa, "yzx".index(qa)).astype(bf16)
    kv_grads = []
    if opt("ou") == 5:
        out_rows = [
            core_sum(matmul(after(hidden, query_grads[0]), w_down_all).astype(bf16)) for hidden in hiddens
        ]
    for b in range(batches):
        if b == batches - 1 and opt("hc"):
            carried[b][0] = after(carried[b][0], *[[], [out_cores, q_cores], [out_cores], [q_cores]][opt("hc")])
        sent = carried[b][0]
        for group in carried[b][1:]:
            sent = (move.hop(sent, "z", -1).astype(f32) + group.astype(f32)).astype(bf16)
        if b == batches - 1:
            sent = after(sent, *([up_total] if opt("s") & 1 else []), *([q_cores] if opt("s") & 2 else []))
        total = sent[0].astype(f32)
        for k in range(1, xs):
            total = total + move.shift(sent[k], "x", -k).astype(f32)
        kv_grads.append(total)
    outputs = [
        (resids[b] + chip_sum(out_rows[b])).astype(bf16) for b in range(batches)
    ]
    kv_grads[-1] = after(
        kv_grads[-1], *([out_chips] if opt("t") & 1 else []), *(outputs if opt("t") & 2 else []),
        *([q_chips] if opt("t") & 4 else []),
    )

    kv_sum = jnp.concatenate(kv_grads, axis=1)
    key_grad, gk_gain = head_backward(
        kv_sum[:KV_WIDTH].reshape(KV_HEADS, HEAD_DIM, both_rows), key_lin, key_scale, gain_k,
        cosine, sine,
    )
    kv_grad = jnp.concatenate(
        [key_grad.astype(bf16).reshape(KV_WIDTH, both_rows), kv_sum[KV_WIDTH:].astype(bf16)],
        axis=0,
    )
    kv_cores = split_cores(dot(normed, kv_grad, 0, 1), d_rows)
    if opt("tl") & 1:
        out_chips = after(out_chips, kv_cores)
    if opt("tl") & 2:
        q_chips = after(q_chips, kv_cores)
    kv_chips = kv_cores
    grad_out_w = move.scatter_chips(out_chips, "xyz".replace(oa, ""))
    grad_q_w = move.scatter_chips(q_chips, "xyz".replace(qa, ""))
    grad_kv_w = move.scatter_chips(kv_chips, opt("kord", "xyz"))
    grad_normed = dot(query_grad, w_q_all, 0, 1) + dot(kv_grad, w_kv_all, 0, 1)
    normed_back = norm_backward(grad_normed, inputs, scale_in)
    token_grads = [
        (grad_resids[b] + normed_back[part]).astype(bf16) for b, part in enumerate(parts)
    ]

    both_sum = jnp.concatenate([gate_sum, up_sum], axis=2).reshape(ys, cs, d_rows, -1)
    if opt("bs"):
        both_sum = after(both_sum, kv_cores)
    both_sum = move.exchange(both_sum, "y", 0, 2)
    both_sum = move.exchange(both_sum, "c", 0, 2).astype(f32)
    grad_gate_w = both_sum[..., :ffn_part].reshape(d_rows, -1)
    grad_up_w = both_sum[..., ffn_part:].reshape(d_rows, -1)

    attn_gain_grad = jnp.sum(grad_q_w * w_query.astype(f32), axis=1) + jnp.sum(
        grad_kv_w * w_kv.astype(f32), axis=1
    )
    ffn_gain_grad = jnp.sum(
        grad_gate_w * w_gate.astype(f32) + grad_up_w * w_up.astype(f32), axis=1
    )
    grad_kv_w = grad_kv_w * gain_a
    small = jnp.concatenate([gq_gain, gk_gain])[None, :]
    if opt("sm"):
        small = after(small, *[[], [kv_cores], [grad_kv_w]][opt("sm")])
    for axis in LAYOUT:
        small = move.total(small, axis)

    return (
        jnp.stack(outputs),
        jnp.stack(token_grads),
        attn_gain_grad,
        grad_q_w * gain_a,
        grad_kv_w[:, :KV_WIDTH],
        grad_kv_w[:, KV_WIDTH:],
        small[0, :HEAD_DIM],
        small[0, HEAD_DIM:],
        grad_out_w,
        ffn_gain_grad,
        grad_gate_w * gain_f,
        grad_up_w * gain_f,
        grad_down,
    )


def solution(mesh):
    sizes = {"c": 2, "z": Z_CHIPS}
    sizes["y"] = mesh.shape["seq"] // sizes["c"]
    sizes["x"] = mesh.shape["ctx"] // sizes["z"]
    grid = Mesh(mesh.devices.reshape([sizes[a] for a in "yczx"]), ("y", "c", "z", "x"))
    seq, ctx, every = ("y", "c"), ("z", "x"), ("y", "c", "z", "x")
    acts, vector, matrix = P(seq, ctx, None), P(every), P(every, None)
    in_specs = (
        acts, acts, P(seq, ctx), P(seq), P(), vector, matrix, matrix, matrix, P(), P(), matrix,
        vector, matrix, matrix, matrix,
    )
    out_specs = (
        acts, acts, vector, matrix, matrix, matrix, P(), P(), matrix, vector, matrix, matrix,
        matrix,
    )
    return jax.shard_map(
        functools.partial(per_device, sizes), mesh=grid, in_specs=in_specs, out_specs=out_specs,
        check_vma=False,
    )
```

```python
import functools
import math

import jax
import jax.numpy as jnp
import numpy as np
from jax import lax
from jax.experimental import pallas as pl
from jax.experimental.pallas import tpu as pltpu
from jax.sharding import Mesh
from jax.sharding import PartitionSpec as P

HEADS = 20
KV_HEADS = 5
GROUP = HEADS // KV_HEADS
HEAD_DIM = 64
TAGS = 4
Q_WIDTH = HEADS * HEAD_DIM
KV_WIDTH = KV_HEADS * HEAD_DIM
DOC_MOST = 1024
Z_CHIPS = 4
EPS = 1e-06
SCORE_SCALE = 0.125
LOG2E = math.log2(math.e)
MASKED = -1e30

bf16 = jnp.bfloat16
f32 = jnp.float32


def dot(left, right, left_dim, right_dim):
    return lax.dot_general(
        left, right, (((left_dim,), (right_dim,)), ((), ())), preferred_element_type=f32
    )


def matmul(left, right):
    return dot(left, right, 1, 0)


def block_slot(block, at_x, xs):
    return (block // xs) * xs + lax.rem(at_x - lax.rem(block, xs) + xs, xs)


def forward_kernel(xs, meta, start_ref, q_ref, k_ref, v_ref, o_ref, lse_ref, bias_ref, q_rows, acc):
    rows = q_ref.shape[1]
    size = k_ref.shape[2]
    low, high, q_start, at_x = meta[0], meta[1], meta[2], meta[3]

    @pl.when(pl.program_id(0) == 0)
    def _():
        q_pos = q_start + lax.broadcasted_iota(jnp.int32, (rows, size), 0)
        lanes = lax.broadcasted_iota(jnp.int32, (rows, size), 1)

        def fill(block, carry):
            key_pos = block * size + lanes
            allowed = (key_pos >= start_ref[...]) & (key_pos <= q_pos)
            bias_ref[block] = jnp.where(allowed, 0.0, MASKED)
            return carry

        lax.fori_loop(low, high, fill, 0)

    q_cols = q_ref[...].T
    for head in range(GROUP):
        q_rows[head] = q_cols[:, head * HEAD_DIM : (head + 1) * HEAD_DIM]
    sub = lax.broadcasted_iota(jnp.int32, (HEAD_DIM, size), 0)
    ones = jnp.where(sub == 0, 1.0, 0.0).astype(bf16)
    acc[...] = jnp.zeros_like(acc)

    def body(block, carry):
        slot = block_slot(block, at_x, xs)
        key_cols = k_ref[slot]
        value_rows = jnp.concatenate([v_ref[slot], ones], axis=0).T
        bias = bias_ref[block]
        for head in range(GROUP):
            raw = jnp.dot(q_rows[head], key_cols, preferred_element_type=f32)
            probs = jnp.exp2(raw * (SCORE_SCALE * LOG2E) + bias).astype(bf16)
            acc[head] += jnp.dot(probs, value_rows, preferred_element_type=f32)
        return carry

    lax.fori_loop(low, high, body, 0)
    for head in range(GROUP):
        turned = acc[head].T
        total = turned[HEAD_DIM : HEAD_DIM + 1, :]
        o_ref[head * HEAD_DIM : (head + 1) * HEAD_DIM, :] = (turned[:HEAD_DIM] / total).astype(bf16)
        lse_ref[0, head : head + 1, :] = jnp.log2(total)


def backward_kernel(
    xs, meta, start_ref, q_ref, k_ref, v_ref, go_ref, o_ref, lse_ref,
    dq_ref, dkv_ref, bias_ref, q_rows, go_rows, dq_acc, delta_ref,
):
    rows = q_ref.shape[1]
    size = k_ref.shape[2]
    low, high, q_start, at_x = meta[0], meta[1], meta[2], meta[3]

    @pl.when(pl.program_id(0) == 0)
    def _():
        q_pos = q_start + lax.broadcasted_iota(jnp.int32, (size, rows), 1)
        subs = lax.broadcasted_iota(jnp.int32, (size, rows), 0)

        def fill(block, carry):
            key_pos = block * size + subs
            allowed = (key_pos >= start_ref[...]) & (key_pos <= q_pos)
            bias_ref[block] = jnp.where(allowed, 0.0, MASKED)
            return carry

        lax.fori_loop(low, high, fill, 0)

    q_cols = q_ref[...].T
    go_cols = go_ref[...].T
    for head in range(GROUP):
        part = slice(head * HEAD_DIM, (head + 1) * HEAD_DIM)
        q_rows[head] = q_cols[:, part]
        go_rows[head] = go_cols[:, part]
        delta_ref[head : head + 1, :] = jnp.sum(
            go_ref[part, :].astype(f32) * o_ref[part, :].astype(f32), axis=0, keepdims=True
        )
    dkv_ref[...] = jnp.zeros_like(dkv_ref)
    dq_acc[...] = jnp.zeros_like(dq_acc)

    def body(block, carry):
        slot = block_slot(block, at_x, xs)
        key_cols = k_ref[slot]
        key_rows = key_cols.T
        value_rows = v_ref[slot].T
        bias = bias_ref[block]
        dk = jnp.zeros((size, HEAD_DIM), f32)
        dv = jnp.zeros((size, HEAD_DIM), f32)
        for head in range(GROUP):
            part = slice(head * HEAD_DIM, (head + 1) * HEAD_DIM)
            raw = jnp.dot(key_rows, q_ref[part, :], preferred_element_type=f32)
            probs = jnp.exp2(
                raw * (SCORE_SCALE * LOG2E) + (bias - lse_ref[0, head : head + 1, :])
            )
            grad_probs = jnp.dot(value_rows, go_ref[part, :], preferred_element_type=f32)
            grad_scores = (probs * (grad_probs - delta_ref[head : head + 1, :])).astype(bf16)
            dv += jnp.dot(probs.astype(bf16), go_rows[head], preferred_element_type=f32)
            dk += jnp.dot(grad_scores, q_rows[head], preferred_element_type=f32)
            dq_acc[part, :] += jnp.dot(key_cols, grad_scores, preferred_element_type=f32)
        dkv_ref[slot, 0] = (SCORE_SCALE * dk).T.astype(bf16)
        dkv_ref[slot, 1] = dv.T.astype(bf16)
        return carry

    lax.fori_loop(low, high, body, 0)
    dq_ref[...] = (SCORE_SCALE * dq_acc[...]).astype(bf16)


def attend_forward(xs, meta, start_col, q_t, batch, window):
    rows = start_col.shape[0]
    blocks, _, size = window.shape
    wide = GROUP * HEAD_DIM
    return pl.pallas_call(
        functools.partial(forward_kernel, xs),
        name="attend_forward",
        grid_spec=pltpu.PrefetchScalarGridSpec(
            num_scalar_prefetch=1,
            grid=(KV_HEADS,),
            in_specs=[
                pl.BlockSpec((rows, 1), lambda g, m: (0, 0)),
                pl.BlockSpec((wide, rows), lambda g, m: (g, batch)),
                pl.BlockSpec((blocks, HEAD_DIM, size), lambda g, m: (0, g, 0)),
                pl.BlockSpec((blocks, HEAD_DIM, size), lambda g, m: (0, KV_HEADS + g, 0)),
            ],
            out_specs=[
                pl.BlockSpec((wide, rows), lambda g, m: (g, 0)),
                pl.BlockSpec((1, GROUP, rows), lambda g, m: (g, 0, 0)),
            ],
            scratch_shapes=[
                pltpu.VMEM((blocks, rows, size), f32),
                pltpu.VMEM((GROUP, rows, HEAD_DIM), bf16),
                pltpu.VMEM((GROUP, rows, 2 * HEAD_DIM), f32),
            ],
        ),
        out_shape=[
            jax.ShapeDtypeStruct((Q_WIDTH, rows), bf16),
            jax.ShapeDtypeStruct((KV_HEADS, GROUP, rows), f32),
        ],
        cost_estimate=pl.CostEstimate(
            flops=4 * HEADS * rows * blocks * size * 128, bytes_accessed=4 * 1024 * 1024,
            transcendentals=HEADS * rows * blocks * size,
        ),
    )(meta, start_col, q_t, window, window)


def attend_backward(xs, meta, start_row, q_t, batch, window, go_t, o_t, lse):
    rows = start_row.shape[1]
    blocks, _, size = window.shape
    wide = GROUP * HEAD_DIM
    return pl.pallas_call(
        functools.partial(backward_kernel, xs),
        name="attend_backward",
        grid_spec=pltpu.PrefetchScalarGridSpec(
            num_scalar_prefetch=1,
            grid=(KV_HEADS,),
            in_specs=[
                pl.BlockSpec((1, rows), lambda g, m: (0, 0)),
                pl.BlockSpec((wide, rows), lambda g, m: (g, batch)),
                pl.BlockSpec((blocks, HEAD_DIM, size), lambda g, m: (0, g, 0)),
                pl.BlockSpec((blocks, HEAD_DIM, size), lambda g, m: (0, KV_HEADS + g, 0)),
                pl.BlockSpec((wide, rows), lambda g, m: (g, 0)),
                pl.BlockSpec((wide, rows), lambda g, m: (g, 0)),
                pl.BlockSpec((1, GROUP, rows), lambda g, m: (g, 0, 0)),
            ],
            out_specs=[
                pl.BlockSpec((wide, rows), lambda g, m: (g, 0)),
                pl.BlockSpec((blocks, 2, HEAD_DIM, size), lambda g, m: (0, 0, g, 0)),
            ],
            scratch_shapes=[
                pltpu.VMEM((blocks, size, rows), f32),
                pltpu.VMEM((GROUP, rows, HEAD_DIM), bf16),
                pltpu.VMEM((GROUP, rows, HEAD_DIM), bf16),
                pltpu.VMEM((wide, rows), f32),
                pltpu.VMEM((8, rows), f32),
            ],
        ),
        out_shape=[
            jax.ShapeDtypeStruct((Q_WIDTH, rows), bf16),
            jax.ShapeDtypeStruct((blocks, 2, KV_WIDTH, size), bf16),
        ],
        cost_estimate=pl.CostEstimate(
            flops=10 * HEADS * rows * blocks * size * 128, bytes_accessed=8 * 1024 * 1024,
            transcendentals=HEADS * rows * blocks * size,
        ),
    )(meta, start_row, q_t, window, window, go_t, o_t, lse)


LAYOUT = "yczx"
CTX = ("z", "x")
DOC_ROWS = 16


def after(value, *earlier):
    return lax.optimization_barrier((value, *earlier))[0]


class Transfers:
    def __init__(self, sizes):
        self.sizes = sizes

    def shift(self, value, axis, step):
        size = self.sizes[axis]
        return lax.ppermute(value, axis, [(i, (i + step) % size) for i in range(size)])

    def hop(self, value, axis, step):
        size = self.sizes[axis]
        pairs = [(i, i + step) for i in range(size) if 0 <= i + step < size]
        return lax.ppermute(value, axis, pairs)

    def place(self, pieces, axis, dim):
        size = self.sizes[axis]
        if size == 1:
            return jnp.expand_dims(pieces[0], dim)
        shape = pieces[0].shape
        rank = len(shape) + 1
        index = lax.broadcasted_iota(
            jnp.int32, tuple(size if d == dim else 1 for d in range(rank)), dim
        )
        back = jnp.mod(lax.axis_index(axis) - index, size)
        whole = jnp.broadcast_to(
            jnp.expand_dims(pieces[0], dim), shape[:dim] + (size,) + shape[dim:]
        )
        for k in range(1, size):
            whole = jnp.where(back == k, jnp.expand_dims(pieces[k], dim), whole)
        return whole

    def ring(self, value, axis):
        pieces = [value]
        for _ in range(1, self.sizes[axis]):
            pieces.append(self.shift(pieces[-1], axis, 1))
        return pieces

    def direct(self, value, axis):
        return [value] + [self.shift(value, axis, k) for k in range(1, self.sizes[axis])]

    def total(self, value, axis):
        size, step = self.sizes[axis], 1
        while step < size:
            value = value + lax.ppermute(value, axis, [(i, i ^ step) for i in range(size)])
            step *= 2
        return value

    def gather(self, value, axis, dim):
        return self.place(self.ring(value, axis), axis, dim)

    def take(self, value, axis, dim, step):
        size = self.sizes[axis]
        index = jnp.mod(lax.axis_index(axis) + step, size)
        return lax.dynamic_index_in_dim(value, index, dim, keepdims=False)

    def scatter(self, value, axis, dim):
        total = self.take(value, axis, dim, 0).astype(f32)
        for k in range(1, self.sizes[axis]):
            sent = self.take(value, axis, dim, k).astype(bf16)
            total = total + self.shift(sent, axis, k).astype(f32)
        return total

    def exchange(self, value, axis, dim, out_dim):
        pieces = [self.take(value, axis, dim, 0)]
        for k in range(1, self.sizes[axis]):
            pieces.append(self.shift(self.take(value, axis, dim, k), axis, k))
        return self.place(pieces, axis, out_dim)

    def spread(self, pieces, order):
        value = self.place(pieces, "z", 0)
        have = ["z"]
        for axis in order:
            dim = sum(1 for a in have if LAYOUT.index(a) < LAYOUT.index(axis))
            value = self.gather(value, axis, dim)
            have.append(axis)
        return value

    def scatter_chips(self, value, order):
        have = [axis for axis in LAYOUT if axis in order]
        for number, axis in enumerate(order):
            value = self.scatter(value, axis, have.index(axis))
            if number < len(order) - 1:
                value = value.astype(bf16)
            have.remove(axis)
        return value


def head_forward(lin, gain, cosine, sine):
    scale = lax.rsqrt(jnp.mean(lin * lin, axis=1, keepdims=True) + EPS)
    normal = lin * scale * gain[None, :, None]
    half = HEAD_DIM // 2
    first, second = normal[:, :half], normal[:, half:]
    turned = jnp.concatenate(
        [first * cosine - second * sine, second * cosine + first * sine], axis=1
    )
    return turned, scale


def head_backward(grad, lin, scale, gain, cosine, sine):
    half = HEAD_DIM // 2
    first, second = grad[:, :half], grad[:, half:]
    back = jnp.concatenate(
        [first * cosine + second * sine, second * cosine - first * sine], axis=1
    )
    gain_grad = jnp.sum(back * lin * scale, axis=(0, 2))
    scaled = back * gain[None, :, None]
    lin_grad = scale * scaled - lin * (scale**3) * jnp.mean(scaled * lin, axis=1, keepdims=True)
    return lin_grad, gain_grad


def row_scale(values):
    return lax.rsqrt(jnp.mean(values * values, axis=-1, keepdims=True) + EPS)


def norm_backward(grad, values, scale):
    return scale * grad - values * (scale**3) * jnp.mean(grad * values, axis=-1, keepdims=True)


def per_device(
    sizes, tokens, out_grad, doc_ids, corpus, corpus_weight, attn_gain, w_query, w_key, w_value,
    query_gain, key_gain, w_out, ffn_gain, w_gate, w_up, w_down,
):
    move = Transfers(sizes)
    ys, cs, zs, xs = (sizes[a] for a in LAYOUT)
    batches, local, width = tokens.shape
    both_rows = batches * local
    span = xs * local
    back_groups = -(-(DOC_MOST - 1) // span)
    at_z, at_x = lax.axis_index("z"), lax.axis_index("x")
    ffn_part = w_gate.shape[1] // (ys * cs)
    d_rows = w_gate.shape[0]
    parts = [slice(b * local, (b + 1) * local) for b in range(batches)]

    gain_a = attn_gain.astype(f32)[:, None]
    gain_f = ffn_gain.astype(f32)[:, None]
    w_kv = jnp.concatenate([w_key, w_value], axis=1)
    kv_near = move.direct((w_kv.astype(f32) * gain_a).astype(bf16), "z")
    w_q_low = (w_query.astype(f32) * gain_a).astype(bf16)
    q_near = move.direct(w_q_low, "z")
    kv_x = move.gather(move.place(kv_near, "z", 0), "x", 1)
    w_kv_all = move.gather(move.gather(kv_x, "y", 0), "c", 1).reshape(width, 2 * KV_WIDTH)

    w_gate_low = (w_gate.astype(f32) * gain_f).astype(bf16).reshape(d_rows, ys, cs, 1, ffn_part)
    w_up_low = (w_up.astype(f32) * gain_f).astype(bf16).reshape(d_rows, ys, cs, 1, ffn_part)
    both = jnp.concatenate([w_gate_low, w_up_low], axis=3).reshape(d_rows, ys, cs, 2 * ffn_part)
    both = move.exchange(after(both, kv_near[0]), "c", 2, 0)
    both = move.exchange(after(both, kv_x), "y", 2, 0)
    both = lax.all_gather(both, CTX, axis=0)
    w_down_all = lax.all_gather(w_down, CTX, axis=0, tiled=True)
    w_both = both.transpose(1, 2, 0, 3, 4).reshape(width, 2 * ffn_part)

    q_start = back_groups * span + at_x * local
    high = back_groups * xs + at_x + 1

    half_dim = HEAD_DIM // 2
    frequency = jnp.exp(
        jnp.arange(half_dim, dtype=f32) * (-2.0 * math.log(10000.0) / HEAD_DIM)
    )
    positions = (at_z * xs + at_x) * local + jnp.arange(local, dtype=jnp.int32)
    angles = frequency[:, None] * jnp.tile(positions, batches).astype(f32)[None, :]
    cosine, sine = jnp.cos(angles)[None], jnp.sin(angles)[None]
    gain_q, gain_k = query_gain.astype(f32), key_gain.astype(f32)

    tag_range = jnp.arange(TAGS, dtype=jnp.int32)
    grads_out = [
        jnp.sum(jnp.where(tag_range == corpus[b], corpus_weight, 0.0)) * out_grad[b].astype(f32)
        for b in range(batches)
    ]

    def core_blocks(chips):
        blocks = list(chips)
        for k in range(1, cs):
            blocks += [move.shift(chip, "c", k) for chip in chips]
        return blocks

    def core_sum(partial):
        blocks = partial.reshape(cs, ys, local, width)
        total = blocks[0].astype(f32)
        for k in range(1, cs):
            total = total + move.shift(blocks[k], "c", -k).astype(f32)
        return [total[0]] + [total[k].astype(bf16) for k in range(1, ys)]

    def chip_sum(rows):
        result = rows[0]
        for k in range(1, ys):
            result = result + move.shift(rows[k], "y", -k).astype(f32)
        return result

    inputs = after(tokens, *kv_near[1:]).reshape(both_rows, width).astype(f32)
    scale_in = row_scale(inputs)
    normed = (inputs * scale_in).astype(bf16)
    kv_lin = dot(w_kv_all, normed, 0, 1)
    key_lin = kv_lin[:KV_WIDTH].reshape(KV_HEADS, HEAD_DIM, both_rows)
    key_rot, key_scale = head_forward(key_lin, gain_k, cosine, sine)
    kv = jnp.concatenate(
        [
            key_rot.astype(bf16).reshape(KV_WIDTH, both_rows),
            kv_lin[KV_WIDTH:].astype(bf16),
            jnp.broadcast_to(doc_ids.reshape(1, both_rows).astype(bf16), (DOC_ROWS, both_rows)),
        ],
        axis=0,
    )
    hops = [kv]
    for _ in range(back_groups):
        hops.append(move.hop(hops[-1], "z", 1))
    w_q_all = move.spread(q_near, "xyc").reshape(width, Q_WIDTH)
    w_out_all = lax.all_gather(w_out, tuple(LAYOUT), axis=0, tiled=True)
    half = Q_WIDTH // 2
    query_lin = jnp.concatenate(
        [dot(w_q_all[:, :half], normed, 0, 1), dot(w_q_all[:, half:], normed, 0, 1)], axis=0
    ).reshape(HEADS, HEAD_DIM, both_rows)
    query_rot, query_scale = head_forward(query_lin, gain_q, cosine, sine)
    query_t = query_rot.astype(bf16).reshape(Q_WIDTH, both_rows)

    grad_chips = move.ring(
        after(jnp.concatenate(grads_out, axis=0).astype(bf16), hops[1]), "y"
    )

    blocks = []
    for group in hops[::-1]:
        blocks += move.direct(group, "x")
    windows = [jnp.stack([block[:, part] for block in blocks]) for part in parts]
    present = at_z + jnp.repeat(jnp.arange(back_groups + 1), xs) >= back_groups
    starts = []
    for b in range(batches):
        docs = jnp.where(present[:, None], windows[b][:, 2 * KV_WIDTH].astype(jnp.int32), -1)
        below = docs.reshape(1, -1) < doc_ids[b][:, None]
        starts.append(jnp.sum(below.astype(jnp.int32), axis=1))

    metas, mixed, lses, resids, scale_mids, normed2_all = [], [], [], [], [], []
    rows, normed2_chips = None, []
    for b, part in enumerate(parts):
        meta = jnp.stack([starts[b][0] // local, high, q_start, at_x]).astype(jnp.int32)
        if rows is not None:
            meta = after(meta, rows)
        mixed_t, lse = attend_forward(xs, meta, starts[b][:, None], query_t, b, windows[b])
        resid = inputs[part] + dot(mixed_t, w_out_all, 0, 0)
        scale_mid = row_scale(resid)
        rows = (resid * scale_mid).astype(bf16)
        normed2_chips.append(move.ring(rows, "y"))
        metas.append(meta)
        mixed.append(mixed_t)
        lses.append(lse)
        resids.append(resid)
        scale_mids.append(scale_mid)

    grad_blocks = core_blocks(grad_chips)
    grads_all = [jnp.concatenate([g[part] for g in grad_blocks], axis=0) for part in parts]

    hidden_grads = [dot(grads, w_down_all, 1, 1) for grads in grads_all]

    hiddens, gate_grads, up_grads, sums = [], [], [], []
    for b in range(batches):
        chips = normed2_chips[b]
        if b > 0:
            chips = chips[:1] + [after(chip, partial) for chip in chips[1:]]
        normed2_all.append(jnp.concatenate(core_blocks(chips), axis=0))
        wide = matmul(normed2_all[b], w_both)
        gate, up = wide[:, :ffn_part], wide[:, ffn_part:]
        sig = jax.nn.sigmoid(gate)
        silu = gate * sig
        hiddens.append((silu * up).astype(bf16))
        grad_hidden = hidden_grads[b]
        if b > 0:
            grad_hidden = after(grad_hidden, *sums[-1][1:])
        grad_gate = (grad_hidden * up * (sig * (1.0 + gate * (1.0 - sig)))).astype(bf16)
        grad_up = (grad_hidden * silu).astype(bf16)
        grad_wide = jnp.concatenate([grad_gate, grad_up], axis=1)
        partial = dot(grad_wide, w_both, 1, 1).astype(bf16)
        sums.append(core_sum(partial))
        gate_grads.append(grad_gate)
        up_grads.append(grad_up)

    grad_resids, low_grads = [], []
    for b in range(batches):
        grad_normed2 = chip_sum(sums[b])
        grad_resid = grads_out[b] + norm_backward(grad_normed2, resids[b], scale_mids[b])
        grad_resids.append(grad_resid)
        low_grads.append(grad_resid.astype(bf16))

    def token_sum(lefts, rights):
        total = dot(lefts[0], rights[0], 0, 0)
        for left, right in zip(lefts[1:], rights[1:]):
            total = total + dot(left, right, 0, 0)
        return total.astype(bf16)

    def scatter_columns(total):
        value = total.reshape(ys * cs, zs * xs * d_rows, ffn_part)
        return lax.psum_scatter(value, CTX, scatter_dimension=1, tiled=True)

    down_total = token_sum([after(hidden, partial) for hidden in hiddens], grads_all)
    grad_down = lax.psum_scatter(down_total, CTX, scatter_dimension=0, tiled=True).astype(f32)

    def split_cores(value, rows):
        value = value.astype(bf16).reshape(ys, cs, zs, xs, rows, -1)
        return move.scatter(value, "c", 1).astype(bf16)

    query_grads, carried = [], []
    for b in range(batches):
        grad_mixed_t = dot(w_out_all, low_grads[b], 1, 1).astype(bf16)
        dq_t, dkv = attend_backward(
            xs, metas[b], starts[b][None, :], query_t, b, windows[b], grad_mixed_t, mixed[b],
            lses[b],
        )
        query_grads.append(dq_t)
        groups = dkv.reshape(back_groups + 1, xs, 2 * KV_WIDTH, local)
        first = (move.hop(groups[0], "z", -1).astype(f32) + groups[1].astype(f32)).astype(bf16)
        carried.append([first] + [groups[k] for k in range(2, back_groups + 1)])

    held = query_grads[0]
    out_cores = split_cores(
        matmul(jnp.concatenate(mixed, axis=1), jnp.concatenate(low_grads, axis=0)), w_out.shape[0]
    )
    gate_total = token_sum(normed2_all, [after(gate_grads[0], held)] + gate_grads[1:])
    gate_sum = scatter_columns(gate_total)

    query_grad, gq_gain = head_backward(
        jnp.concatenate(query_grads, axis=1).astype(f32).reshape(HEADS, HEAD_DIM, both_rows),
        query_lin, query_scale, gain_q, cosine, sine,
    )
    query_grad = query_grad.astype(bf16).reshape(Q_WIDTH, both_rows)
    q_cores = split_cores(dot(normed, query_grad, 0, 1), d_rows)

    up_total = token_sum(normed2_all, [after(up_grads[0], held)] + up_grads[1:])
    up_sum = scatter_columns(up_total)

    out_chips = move.scatter(out_cores, "y", 0).astype(bf16)
    q_chips = move.scatter(q_cores, "x", 2).astype(bf16)
    out_rows = [
        core_sum(matmul(after(hidden, held), w_down_all).astype(bf16)) for hidden in hiddens
    ]
    kv_grads = []
    for b in range(batches):
        sent = carried[b][0]
        if b == batches - 1:
            sent = after(sent, out_cores, q_cores)
        for group in carried[b][1:]:
            sent = (move.hop(sent, "z", -1).astype(f32) + group.astype(f32)).astype(bf16)
        total = sent[0].astype(f32)
        for k in range(1, xs):
            total = total + move.shift(sent[k], "x", -k).astype(f32)
        kv_grads.append(total)
    outputs = [
        (resids[b] + chip_sum(out_rows[b])).astype(bf16) for b in range(batches)
    ]

    kv_sum = jnp.concatenate(kv_grads, axis=1)
    key_grad, gk_gain = head_backward(
        kv_sum[:KV_WIDTH].reshape(KV_HEADS, HEAD_DIM, both_rows), key_lin, key_scale, gain_k,
        cosine, sine,
    )
    kv_grad = jnp.concatenate(
        [key_grad.astype(bf16).reshape(KV_WIDTH, both_rows), kv_sum[KV_WIDTH:].astype(bf16)],
        axis=0,
    )
    kv_cores = split_cores(dot(normed, kv_grad, 0, 1), d_rows)
    grad_out_w = move.scatter_chips(after(out_chips, kv_cores), "xz")
    grad_q_w = move.scatter_chips(after(q_chips, kv_cores), "yz")
    grad_kv_w = move.scatter_chips(kv_cores, "xyz")
    grad_normed = dot(query_grad, w_q_all, 0, 1) + dot(kv_grad, w_kv_all, 0, 1)
    normed_back = norm_backward(grad_normed, inputs, scale_in)
    token_grads = [
        (grad_resids[b] + normed_back[part]).astype(bf16) for b, part in enumerate(parts)
    ]

    both_sum = jnp.concatenate([gate_sum, up_sum], axis=2).reshape(ys, cs, d_rows, -1)
    both_sum = move.exchange(after(both_sum, kv_cores), "y", 0, 2)
    both_sum = move.exchange(both_sum, "c", 0, 2).astype(f32)
    grad_gate_w = both_sum[..., :ffn_part].reshape(d_rows, -1)
    grad_up_w = both_sum[..., ffn_part:].reshape(d_rows, -1)

    attn_gain_grad = jnp.sum(grad_q_w * w_query.astype(f32), axis=1) + jnp.sum(
        grad_kv_w * w_kv.astype(f32), axis=1
    )
    ffn_gain_grad = jnp.sum(
        grad_gate_w * w_gate.astype(f32) + grad_up_w * w_up.astype(f32), axis=1
    )
    grad_kv_w = grad_kv_w * gain_a
    small = after(jnp.concatenate([gq_gain, gk_gain])[None, :], kv_cores)
    for axis in LAYOUT:
        small = move.total(small, axis)

    return (
        jnp.stack(outputs),
        jnp.stack(token_grads),
        attn_gain_grad,
        grad_q_w * gain_a,
        grad_kv_w[:, :KV_WIDTH],
        grad_kv_w[:, KV_WIDTH:],
        small[0, :HEAD_DIM],
        small[0, HEAD_DIM:],
        grad_out_w,
        ffn_gain_grad,
        grad_gate_w * gain_f,
        grad_up_w * gain_f,
        grad_down,
    )


def solution(mesh):
    sizes = {"c": 2, "z": Z_CHIPS}
    sizes["y"] = mesh.shape["seq"] // sizes["c"]
    sizes["x"] = mesh.shape["ctx"] // sizes["z"]
    grid = Mesh(mesh.devices.reshape([sizes[a] for a in "yczx"]), ("y", "c", "z", "x"))
    seq, ctx, every = ("y", "c"), ("z", "x"), ("y", "c", "z", "x")
    acts, vector, matrix = P(seq, ctx, None), P(every), P(every, None)
    in_specs = (
        acts, acts, P(seq, ctx), P(seq), P(), vector, matrix, matrix, matrix, P(), P(), matrix,
        vector, matrix, matrix, matrix,
    )
    out_specs = (
        acts, acts, vector, matrix, matrix, matrix, P(), P(), matrix, vector, matrix, matrix,
        matrix,
    )
    return jax.shard_map(
        functools.partial(per_device, sizes), mesh=grid, in_specs=in_specs, out_specs=out_specs,
        check_vma=False,
    )
```

```python
import functools
import math

import jax
import jax.numpy as jnp
import numpy as np
from jax import lax
from jax.experimental import pallas as pl
from jax.experimental.pallas import tpu as pltpu
from jax.sharding import Mesh
from jax.sharding import PartitionSpec as P

HEADS = 20
KV_HEADS = 5
GROUP = HEADS // KV_HEADS
HEAD_DIM = 64
TAGS = 4
Q_WIDTH = HEADS * HEAD_DIM
KV_WIDTH = KV_HEADS * HEAD_DIM
DOC_MOST = 1024
Z_CHIPS = 4
EPS = 1e-06
SCORE_SCALE = 0.125
LOG2E = math.log2(math.e)
MASKED = -1e30

bf16 = jnp.bfloat16
f32 = jnp.float32


def dot(left, right, left_dim, right_dim):
    return lax.dot_general(
        left, right, (((left_dim,), (right_dim,)), ((), ())), preferred_element_type=f32
    )


def matmul(left, right):
    return dot(left, right, 1, 0)


def block_slot(block, at_x, xs):
    return (block // xs) * xs + lax.rem(at_x - lax.rem(block, xs) + xs, xs)


def forward_kernel(xs, meta, start_ref, q_ref, k_ref, v_ref, o_ref, lse_ref, bias_ref, q_rows, acc):
    rows = q_ref.shape[1]
    size = k_ref.shape[2]
    low, high, q_start, at_x = meta[0], meta[1], meta[2], meta[3]

    @pl.when(pl.program_id(0) == 0)
    def _():
        q_pos = q_start + lax.broadcasted_iota(jnp.int32, (rows, size), 0)
        lanes = lax.broadcasted_iota(jnp.int32, (rows, size), 1)

        def fill(block, carry):
            key_pos = block * size + lanes
            allowed = (key_pos >= start_ref[...]) & (key_pos <= q_pos)
            bias_ref[block] = jnp.where(allowed, 0.0, MASKED)
            return carry

        lax.fori_loop(low, high, fill, 0)

    q_cols = q_ref[...].T
    for head in range(GROUP):
        q_rows[head] = q_cols[:, head * HEAD_DIM : (head + 1) * HEAD_DIM]
    sub = lax.broadcasted_iota(jnp.int32, (HEAD_DIM, size), 0)
    ones = jnp.where(sub == 0, 1.0, 0.0).astype(bf16)
    acc[...] = jnp.zeros_like(acc)

    def body(block, carry):
        slot = block_slot(block, at_x, xs)
        key_cols = k_ref[slot]
        value_rows = jnp.concatenate([v_ref[slot], ones], axis=0).T
        bias = bias_ref[block]
        for head in range(GROUP):
            raw = jnp.dot(q_rows[head], key_cols, preferred_element_type=f32)
            probs = jnp.exp2(raw * (SCORE_SCALE * LOG2E) + bias).astype(bf16)
            acc[head] += jnp.dot(probs, value_rows, preferred_element_type=f32)
        return carry

    lax.fori_loop(low, high, body, 0)
    for head in range(GROUP):
        turned = acc[head].T
        total = turned[HEAD_DIM : HEAD_DIM + 1, :]
        o_ref[head * HEAD_DIM : (head + 1) * HEAD_DIM, :] = (turned[:HEAD_DIM] / total).astype(bf16)
        lse_ref[0, head : head + 1, :] = jnp.log2(total)


def backward_kernel(
    xs, meta, start_ref, q_ref, k_ref, v_ref, go_ref, o_ref, lse_ref,
    dq_ref, dkv_ref, bias_ref, q_rows, go_rows, dq_acc, delta_ref,
):
    rows = q_ref.shape[1]
    size = k_ref.shape[2]
    low, high, q_start, at_x = meta[0], meta[1], meta[2], meta[3]

    @pl.when(pl.program_id(0) == 0)
    def _():
        q_pos = q_start + lax.broadcasted_iota(jnp.int32, (size, rows), 1)
        subs = lax.broadcasted_iota(jnp.int32, (size, rows), 0)

        def fill(block, carry):
            key_pos = block * size + subs
            allowed = (key_pos >= start_ref[...]) & (key_pos <= q_pos)
            bias_ref[block] = jnp.where(allowed, 0.0, MASKED)
            return carry

        lax.fori_loop(low, high, fill, 0)

    q_cols = q_ref[...].T
    go_cols = go_ref[...].T
    for head in range(GROUP):
        part = slice(head * HEAD_DIM, (head + 1) * HEAD_DIM)
        q_rows[head] = q_cols[:, part]
        go_rows[head] = go_cols[:, part]
        delta_ref[head : head + 1, :] = jnp.sum(
            go_ref[part, :].astype(f32) * o_ref[part, :].astype(f32), axis=0, keepdims=True
        )
    dkv_ref[...] = jnp.zeros_like(dkv_ref)
    dq_acc[...] = jnp.zeros_like(dq_acc)

    def body(block, carry):
        slot = block_slot(block, at_x, xs)
        key_cols = k_ref[slot]
        key_rows = key_cols.T
        value_rows = v_ref[slot].T
        bias = bias_ref[block]
        dk = jnp.zeros((size, HEAD_DIM), f32)
        dv = jnp.zeros((size, HEAD_DIM), f32)
        for head in range(GROUP):
            part = slice(head * HEAD_DIM, (head + 1) * HEAD_DIM)
            raw = jnp.dot(key_rows, q_ref[part, :], preferred_element_type=f32)
            probs = jnp.exp2(
                raw * (SCORE_SCALE * LOG2E) + (bias - lse_ref[0, head : head + 1, :])
            )
            grad_probs = jnp.dot(value_rows, go_ref[part, :], preferred_element_type=f32)
            grad_scores = (probs * (grad_probs - delta_ref[head : head + 1, :])).astype(bf16)
            dv += jnp.dot(probs.astype(bf16), go_rows[head], preferred_element_type=f32)
            dk += jnp.dot(grad_scores, q_rows[head], preferred_element_type=f32)
            dq_acc[part, :] += jnp.dot(key_cols, grad_scores, preferred_element_type=f32)
        dkv_ref[slot, 0] = (SCORE_SCALE * dk).T.astype(bf16)
        dkv_ref[slot, 1] = dv.T.astype(bf16)
        return carry

    lax.fori_loop(low, high, body, 0)
    dq_ref[...] = (SCORE_SCALE * dq_acc[...]).astype(bf16)


def attend_forward(xs, meta, start_col, q_t, batch, window):
    rows = start_col.shape[0]
    blocks, _, size = window.shape
    wide = GROUP * HEAD_DIM
    return pl.pallas_call(
        functools.partial(forward_kernel, xs),
        name="attend_forward",
        grid_spec=pltpu.PrefetchScalarGridSpec(
            num_scalar_prefetch=1,
            grid=(KV_HEADS,),
            in_specs=[
                pl.BlockSpec((rows, 1), lambda g, m: (0, 0)),
                pl.BlockSpec((wide, rows), lambda g, m: (g, batch)),
                pl.BlockSpec((blocks, HEAD_DIM, size), lambda g, m: (0, g, 0)),
                pl.BlockSpec((blocks, HEAD_DIM, size), lambda g, m: (0, KV_HEADS + g, 0)),
            ],
            out_specs=[
                pl.BlockSpec((wide, rows), lambda g, m: (g, 0)),
                pl.BlockSpec((1, GROUP, rows), lambda g, m: (g, 0, 0)),
            ],
            scratch_shapes=[
                pltpu.VMEM((blocks, rows, size), f32),
                pltpu.VMEM((GROUP, rows, HEAD_DIM), bf16),
                pltpu.VMEM((GROUP, rows, 2 * HEAD_DIM), f32),
            ],
        ),
        out_shape=[
            jax.ShapeDtypeStruct((Q_WIDTH, rows), bf16),
            jax.ShapeDtypeStruct((KV_HEADS, GROUP, rows), f32),
        ],
        cost_estimate=pl.CostEstimate(
            flops=4 * HEADS * rows * blocks * size * 128, bytes_accessed=4 * 1024 * 1024,
            transcendentals=HEADS * rows * blocks * size,
        ),
    )(meta, start_col, q_t, window, window)


def attend_backward(xs, meta, start_row, q_t, batch, window, go_t, o_t, lse):
    rows = start_row.shape[1]
    blocks, _, size = window.shape
    wide = GROUP * HEAD_DIM
    return pl.pallas_call(
        functools.partial(backward_kernel, xs),
        name="attend_backward",
        grid_spec=pltpu.PrefetchScalarGridSpec(
            num_scalar_prefetch=1,
            grid=(KV_HEADS,),
            in_specs=[
                pl.BlockSpec((1, rows), lambda g, m: (0, 0)),
                pl.BlockSpec((wide, rows), lambda g, m: (g, batch)),
                pl.BlockSpec((blocks, HEAD_DIM, size), lambda g, m: (0, g, 0)),
                pl.BlockSpec((blocks, HEAD_DIM, size), lambda g, m: (0, KV_HEADS + g, 0)),
                pl.BlockSpec((wide, rows), lambda g, m: (g, 0)),
                pl.BlockSpec((wide, rows), lambda g, m: (g, 0)),
                pl.BlockSpec((1, GROUP, rows), lambda g, m: (g, 0, 0)),
            ],
            out_specs=[
                pl.BlockSpec((wide, rows), lambda g, m: (g, 0)),
                pl.BlockSpec((blocks, 2, HEAD_DIM, size), lambda g, m: (0, 0, g, 0)),
            ],
            scratch_shapes=[
                pltpu.VMEM((blocks, size, rows), f32),
                pltpu.VMEM((GROUP, rows, HEAD_DIM), bf16),
                pltpu.VMEM((GROUP, rows, HEAD_DIM), bf16),
                pltpu.VMEM((wide, rows), f32),
                pltpu.VMEM((8, rows), f32),
            ],
        ),
        out_shape=[
            jax.ShapeDtypeStruct((Q_WIDTH, rows), bf16),
            jax.ShapeDtypeStruct((blocks, 2, KV_WIDTH, size), bf16),
        ],
        cost_estimate=pl.CostEstimate(
            flops=10 * HEADS * rows * blocks * size * 128, bytes_accessed=8 * 1024 * 1024,
            transcendentals=HEADS * rows * blocks * size,
        ),
    )(meta, start_row, q_t, window, window, go_t, o_t, lse)


LAYOUT = "yczx"
CTX = ("z", "x")
DOC_ROWS = 16


def after(value, *earlier):
    return lax.optimization_barrier((value, *earlier))[0]


class Transfers:
    def __init__(self, sizes):
        self.sizes = sizes

    def shift(self, value, axis, step):
        size = self.sizes[axis]
        return lax.ppermute(value, axis, [(i, (i + step) % size) for i in range(size)])

    def hop(self, value, axis, step):
        size = self.sizes[axis]
        pairs = [(i, i + step) for i in range(size) if 0 <= i + step < size]
        return lax.ppermute(value, axis, pairs)

    def place(self, pieces, axis, dim):
        size = self.sizes[axis]
        if size == 1:
            return jnp.expand_dims(pieces[0], dim)
        shape = pieces[0].shape
        rank = len(shape) + 1
        index = lax.broadcasted_iota(
            jnp.int32, tuple(size if d == dim else 1 for d in range(rank)), dim
        )
        back = jnp.mod(lax.axis_index(axis) - index, size)
        whole = jnp.broadcast_to(
            jnp.expand_dims(pieces[0], dim), shape[:dim] + (size,) + shape[dim:]
        )
        for k in range(1, size):
            whole = jnp.where(back == k, jnp.expand_dims(pieces[k], dim), whole)
        return whole

    def ring(self, value, axis):
        pieces = [value]
        for _ in range(1, self.sizes[axis]):
            pieces.append(self.shift(pieces[-1], axis, 1))
        return pieces

    def direct(self, value, axis):
        return [value] + [self.shift(value, axis, k) for k in range(1, self.sizes[axis])]

    def total(self, value, axis):
        size, step = self.sizes[axis], 1
        while step < size:
            value = value + lax.ppermute(value, axis, [(i, i ^ step) for i in range(size)])
            step *= 2
        return value

    def gather(self, value, axis, dim):
        return self.place(self.ring(value, axis), axis, dim)

    def take(self, value, axis, dim, step):
        size = self.sizes[axis]
        index = jnp.mod(lax.axis_index(axis) + step, size)
        return lax.dynamic_index_in_dim(value, index, dim, keepdims=False)

    def scatter(self, value, axis, dim):
        total = self.take(value, axis, dim, 0).astype(f32)
        for k in range(1, self.sizes[axis]):
            sent = self.take(value, axis, dim, k).astype(bf16)
            total = total + self.shift(sent, axis, k).astype(f32)
        return total

    def exchange(self, value, axis, dim, out_dim):
        pieces = [self.take(value, axis, dim, 0)]
        for k in range(1, self.sizes[axis]):
            pieces.append(self.shift(self.take(value, axis, dim, k), axis, k))
        return self.place(pieces, axis, out_dim)

    def spread(self, pieces, order):
        value = self.place(pieces, "z", 0)
        have = ["z"]
        for axis in order:
            dim = sum(1 for a in have if LAYOUT.index(a) < LAYOUT.index(axis))
            value = self.gather(value, axis, dim)
            have.append(axis)
        return value

    def scatter_chips(self, value, order):
        have = [axis for axis in LAYOUT if axis in order]
        for number, axis in enumerate(order):
            value = self.scatter(value, axis, have.index(axis))
            if number < len(order) - 1:
                value = value.astype(bf16)
            have.remove(axis)
        return value


def head_forward(lin, gain, cosine, sine):
    scale = lax.rsqrt(jnp.mean(lin * lin, axis=1, keepdims=True) + EPS)
    normal = lin * scale * gain[None, :, None]
    half = HEAD_DIM // 2
    first, second = normal[:, :half], normal[:, half:]
    turned = jnp.concatenate(
        [first * cosine - second * sine, second * cosine + first * sine], axis=1
    )
    return turned, scale


def head_backward(grad, lin, scale, gain, cosine, sine):
    half = HEAD_DIM // 2
    first, second = grad[:, :half], grad[:, half:]
    back = jnp.concatenate(
        [first * cosine + second * sine, second * cosine - first * sine], axis=1
    )
    gain_grad = jnp.sum(back * lin * scale, axis=(0, 2))
    scaled = back * gain[None, :, None]
    lin_grad = scale * scaled - lin * (scale**3) * jnp.mean(scaled * lin, axis=1, keepdims=True)
    return lin_grad, gain_grad


def row_scale(values):
    return lax.rsqrt(jnp.mean(values * values, axis=-1, keepdims=True) + EPS)


def norm_backward(grad, values, scale):
    return scale * grad - values * (scale**3) * jnp.mean(grad * values, axis=-1, keepdims=True)


def per_device(
    sizes, tokens, out_grad, doc_ids, corpus, corpus_weight, attn_gain, w_query, w_key, w_value,
    query_gain, key_gain, w_out, ffn_gain, w_gate, w_up, w_down,
):
    move = Transfers(sizes)
    ys, cs, zs, xs = (sizes[a] for a in LAYOUT)
    batches, local, width = tokens.shape
    both_rows = batches * local
    span = xs * local
    back_groups = -(-(DOC_MOST - 1) // span)
    at_z, at_x = lax.axis_index("z"), lax.axis_index("x")
    ffn_part = w_gate.shape[1] // (ys * cs)
    d_rows = w_gate.shape[0]
    parts = [slice(b * local, (b + 1) * local) for b in range(batches)]

    gain_a = attn_gain.astype(f32)[:, None]
    gain_f = ffn_gain.astype(f32)[:, None]
    w_kv = jnp.concatenate([w_key, w_value], axis=1)
    kv_near = move.direct((w_kv.astype(f32) * gain_a).astype(bf16), "z")
    w_q_low = (w_query.astype(f32) * gain_a).astype(bf16)
    q_near = move.direct(w_q_low, "z")
    kv_x = move.gather(move.place(kv_near, "z", 0), "x", 1)
    w_kv_all = move.gather(move.gather(kv_x, "y", 0), "c", 1).reshape(width, 2 * KV_WIDTH)

    w_gate_low = (w_gate.astype(f32) * gain_f).astype(bf16).reshape(d_rows, ys, cs, 1, ffn_part)
    w_up_low = (w_up.astype(f32) * gain_f).astype(bf16).reshape(d_rows, ys, cs, 1, ffn_part)
    both = jnp.concatenate([w_gate_low, w_up_low], axis=3).reshape(d_rows, ys, cs, 2 * ffn_part)
    both = move.exchange(after(both, kv_near[0]), "c", 2, 0)
    both = move.exchange(after(both, kv_x), "y", 2, 0)
    both = lax.all_gather(both, CTX, axis=0)
    w_down_all = lax.all_gather(w_down, CTX, axis=0, tiled=True)
    w_both = both.transpose(1, 2, 0, 3, 4).reshape(width, 2 * ffn_part)

    q_start = back_groups * span + at_x * local
    high = back_groups * xs + at_x + 1

    half_dim = HEAD_DIM // 2
    frequency = jnp.exp(
        jnp.arange(half_dim, dtype=f32) * (-2.0 * math.log(10000.0) / HEAD_DIM)
    )
    positions = (at_z * xs + at_x) * local + jnp.arange(local, dtype=jnp.int32)
    angles = frequency[:, None] * jnp.tile(positions, batches).astype(f32)[None, :]
    cosine, sine = jnp.cos(angles)[None], jnp.sin(angles)[None]
    gain_q, gain_k = query_gain.astype(f32), key_gain.astype(f32)

    tag_range = jnp.arange(TAGS, dtype=jnp.int32)
    grads_out = [
        jnp.sum(jnp.where(tag_range == corpus[b], corpus_weight, 0.0)) * out_grad[b].astype(f32)
        for b in range(batches)
    ]

    def core_blocks(chips):
        blocks = list(chips)
        for k in range(1, cs):
            blocks += [move.shift(chip, "c", k) for chip in chips]
        return blocks

    def core_sum(partial):
        blocks = partial.reshape(cs, ys, local, width)
        total = blocks[0].astype(f32)
        for k in range(1, cs):
            total = total + move.shift(blocks[k], "c", -k).astype(f32)
        return [total[0]] + [total[k].astype(bf16) for k in range(1, ys)]

    def chip_sum(rows):
        result = rows[0]
        for k in range(1, ys):
            result = result + move.shift(rows[k], "y", -k).astype(f32)
        return result

    inputs = after(tokens, *kv_near[1:]).reshape(both_rows, width).astype(f32)
    scale_in = row_scale(inputs)
    normed = (inputs * scale_in).astype(bf16)
    kv_lin = dot(w_kv_all, normed, 0, 1)
    key_lin = kv_lin[:KV_WIDTH].reshape(KV_HEADS, HEAD_DIM, both_rows)
    key_rot, key_scale = head_forward(key_lin, gain_k, cosine, sine)
    kv = jnp.concatenate(
        [
            key_rot.astype(bf16).reshape(KV_WIDTH, both_rows),
            kv_lin[KV_WIDTH:].astype(bf16),
            jnp.broadcast_to(doc_ids.reshape(1, both_rows).astype(bf16), (DOC_ROWS, both_rows)),
        ],
        axis=0,
    )
    hops = [kv]
    for _ in range(back_groups):
        hops.append(move.hop(hops[-1], "z", 1))
    w_q_all = move.spread(q_near, "xyc").reshape(width, Q_WIDTH)
    w_out_all = lax.all_gather(w_out, tuple(LAYOUT), axis=0, tiled=True)
    half = Q_WIDTH // 2
    query_lin = jnp.concatenate(
        [dot(w_q_all[:, :half], normed, 0, 1), dot(w_q_all[:, half:], normed, 0, 1)], axis=0
    ).reshape(HEADS, HEAD_DIM, both_rows)
    query_rot, query_scale = head_forward(query_lin, gain_q, cosine, sine)
    query_t = query_rot.astype(bf16).reshape(Q_WIDTH, both_rows)

    grad_chips = move.ring(
        after(jnp.concatenate(grads_out, axis=0).astype(bf16), hops[1]), "y"
    )

    blocks = []
    for group in hops[::-1]:
        blocks += move.direct(group, "x")
    windows = [jnp.stack([block[:, part] for block in blocks]) for part in parts]
    present = at_z + jnp.repeat(jnp.arange(back_groups + 1), xs) >= back_groups
    starts = []
    for b in range(batches):
        docs = jnp.where(present[:, None], windows[b][:, 2 * KV_WIDTH].astype(jnp.int32), -1)
        below = docs.reshape(1, -1) < doc_ids[b][:, None]
        starts.append(jnp.sum(below.astype(jnp.int32), axis=1))

    metas, mixed, lses, resids, scale_mids, normed2_all = [], [], [], [], [], []
    rows, normed2_chips = None, []
    for b, part in enumerate(parts):
        meta = jnp.stack([starts[b][0] // local, high, q_start, at_x]).astype(jnp.int32)
        if rows is not None:
            meta = after(meta, rows)
        mixed_t, lse = attend_forward(xs, meta, starts[b][:, None], query_t, b, windows[b])
        resid = inputs[part] + dot(mixed_t, w_out_all, 0, 0)
        scale_mid = row_scale(resid)
        rows = (resid * scale_mid).astype(bf16)
        normed2_chips.append(move.ring(rows, "y"))
        metas.append(meta)
        mixed.append(mixed_t)
        lses.append(lse)
        resids.append(resid)
        scale_mids.append(scale_mid)

    grad_blocks = core_blocks(grad_chips)
    grads_all = [jnp.concatenate([g[part] for g in grad_blocks], axis=0) for part in parts]

    hidden_grads = [dot(grads, w_down_all, 1, 1) for grads in grads_all]

    hiddens, gate_grads, up_grads, sums = [], [], [], []
    for b in range(batches):
        chips = normed2_chips[b]
        if b > 0:
            chips = chips[:1] + [after(chip, partial) for chip in chips[1:]]
        normed2_all.append(jnp.concatenate(core_blocks(chips), axis=0))
        wide = matmul(normed2_all[b], w_both)
        gate, up = wide[:, :ffn_part], wide[:, ffn_part:]
        sig = jax.nn.sigmoid(gate)
        silu = gate * sig
        hiddens.append((silu * up).astype(bf16))
        grad_hidden = hidden_grads[b]
        if b > 0:
            grad_hidden = after(grad_hidden, *sums[-1][1:])
        grad_gate = (grad_hidden * up * (sig * (1.0 + gate * (1.0 - sig)))).astype(bf16)
        grad_up = (grad_hidden * silu).astype(bf16)
        grad_wide = jnp.concatenate([grad_gate, grad_up], axis=1)
        partial = dot(grad_wide, w_both, 1, 1).astype(bf16)
        sums.append(core_sum(partial))
        gate_grads.append(grad_gate)
        up_grads.append(grad_up)

    grad_resids, low_grads = [], []
    for b in range(batches):
        grad_normed2 = chip_sum(sums[b])
        grad_resid = grads_out[b] + norm_backward(grad_normed2, resids[b], scale_mids[b])
        grad_resids.append(grad_resid)
        low_grads.append(grad_resid.astype(bf16))

    def token_sum(lefts, rights):
        total = dot(lefts[0], rights[0], 0, 0)
        for left, right in zip(lefts[1:], rights[1:]):
            total = total + dot(left, right, 0, 0)
        return total.astype(bf16)

    def scatter_columns(total):
        value = total.reshape(ys * cs, zs * xs * d_rows, ffn_part)
        return lax.psum_scatter(value, CTX, scatter_dimension=1, tiled=True)

    down_total = token_sum([after(hidden, partial) for hidden in hiddens], grads_all)
    grad_down = lax.psum_scatter(down_total, CTX, scatter_dimension=0, tiled=True).astype(f32)

    def split_cores(value, rows):
        value = value.astype(bf16).reshape(ys, cs, zs, xs, rows, -1)
        return move.scatter(value, "c", 1).astype(bf16)

    query_grads, carried = [], []
    for b in range(batches):
        grad_mixed_t = dot(w_out_all, low_grads[b], 1, 1).astype(bf16)
        dq_t, dkv = attend_backward(
            xs, metas[b], starts[b][None, :], query_t, b, windows[b], grad_mixed_t, mixed[b],
            lses[b],
        )
        query_grads.append(dq_t)
        groups = dkv.reshape(back_groups + 1, xs, 2 * KV_WIDTH, local)
        first = (move.hop(groups[0], "z", -1).astype(f32) + groups[1].astype(f32)).astype(bf16)
        carried.append([first] + [groups[k] for k in range(2, back_groups + 1)])

    held = query_grads[0]
    out_cores = split_cores(
        matmul(jnp.concatenate(mixed, axis=1), jnp.concatenate(low_grads, axis=0)), w_out.shape[0]
    )
    gate_total = token_sum(normed2_all, [after(gate_grads[0], held)] + gate_grads[1:])
    gate_sum = scatter_columns(gate_total)

    query_grad, gq_gain = head_backward(
        jnp.concatenate(query_grads, axis=1).astype(f32).reshape(HEADS, HEAD_DIM, both_rows),
        query_lin, query_scale, gain_q, cosine, sine,
    )
    query_grad = query_grad.astype(bf16).reshape(Q_WIDTH, both_rows)
    q_cores = split_cores(dot(normed, query_grad, 0, 1), d_rows)

    up_total = token_sum(normed2_all, [after(up_grads[0], held)] + up_grads[1:])
    up_sum = scatter_columns(up_total)

    out_chips = move.scatter(out_cores, "x", 2).astype(bf16)
    q_chips = move.scatter(q_cores, "y", 0).astype(bf16)
    out_rows = [
        core_sum(matmul(after(hidden, held), w_down_all).astype(bf16)) for hidden in hiddens
    ]
    kv_grads = []
    for b in range(batches):
        sent = carried[b][0]
        if b == batches - 1:
            sent = after(sent, out_cores, q_cores)
        for group in carried[b][1:]:
            sent = (move.hop(sent, "z", -1).astype(f32) + group.astype(f32)).astype(bf16)
        total = sent[0].astype(f32)
        for k in range(1, xs):
            total = total + move.shift(sent[k], "x", -k).astype(f32)
        kv_grads.append(total)
    outputs = [
        (resids[b] + chip_sum(out_rows[b])).astype(bf16) for b in range(batches)
    ]

    kv_sum = jnp.concatenate(kv_grads, axis=1)
    key_grad, gk_gain = head_backward(
        kv_sum[:KV_WIDTH].reshape(KV_HEADS, HEAD_DIM, both_rows), key_lin, key_scale, gain_k,
        cosine, sine,
    )
    kv_grad = jnp.concatenate(
        [key_grad.astype(bf16).reshape(KV_WIDTH, both_rows), kv_sum[KV_WIDTH:].astype(bf16)],
        axis=0,
    )
    kv_cores = split_cores(dot(normed, kv_grad, 0, 1), d_rows)
    grad_out_w = move.scatter_chips(after(out_chips, kv_cores), "yz")
    grad_q_w = move.scatter_chips(after(q_chips, kv_cores), "xz")
    grad_kv_w = move.scatter_chips(kv_cores, "yxz")
    grad_normed = dot(query_grad, w_q_all, 0, 1) + dot(kv_grad, w_kv_all, 0, 1)
    normed_back = norm_backward(grad_normed, inputs, scale_in)
    token_grads = [
        (grad_resids[b] + normed_back[part]).astype(bf16) for b, part in enumerate(parts)
    ]

    both_sum = jnp.concatenate([gate_sum, up_sum], axis=2).reshape(ys, cs, d_rows, -1)
    both_sum = move.exchange(after(both_sum, kv_cores), "y", 0, 2)
    both_sum = move.exchange(both_sum, "c", 0, 2).astype(f32)
    grad_gate_w = both_sum[..., :ffn_part].reshape(d_rows, -1)
    grad_up_w = both_sum[..., ffn_part:].reshape(d_rows, -1)

    attn_gain_grad = jnp.sum(grad_q_w * w_query.astype(f32), axis=1) + jnp.sum(
        grad_kv_w * w_kv.astype(f32), axis=1
    )
    ffn_gain_grad = jnp.sum(
        grad_gate_w * w_gate.astype(f32) + grad_up_w * w_up.astype(f32), axis=1
    )
    grad_kv_w = grad_kv_w * gain_a
    small = after(jnp.concatenate([gq_gain, gk_gain])[None, :], kv_cores)
    for axis in "xyzc":
        small = move.total(small, axis)

    return (
        jnp.stack(outputs),
        jnp.stack(token_grads),
        attn_gain_grad,
        grad_q_w * gain_a,
        grad_kv_w[:, :KV_WIDTH],
        grad_kv_w[:, KV_WIDTH:],
        small[0, :HEAD_DIM],
        small[0, HEAD_DIM:],
        grad_out_w,
        ffn_gain_grad,
        grad_gate_w * gain_f,
        grad_up_w * gain_f,
        grad_down,
    )


def solution(mesh):
    sizes = {"c": 2, "z": Z_CHIPS}
    sizes["y"] = mesh.shape["seq"] // sizes["c"]
    sizes["x"] = mesh.shape["ctx"] // sizes["z"]
    grid = Mesh(mesh.devices.reshape([sizes[a] for a in "yczx"]), ("y", "c", "z", "x"))
    seq, ctx, every = ("y", "c"), ("z", "x"), ("y", "c", "z", "x")
    acts, vector, matrix = P(seq, ctx, None), P(every), P(every, None)
    in_specs = (
        acts, acts, P(seq, ctx), P(seq), P(), vector, matrix, matrix, matrix, P(), P(), matrix,
        vector, matrix, matrix, matrix,
    )
    out_specs = (
        acts, acts, vector, matrix, matrix, matrix, P(), P(), matrix, vector, matrix, matrix,
        matrix,
    )
    return jax.shard_map(
        functools.partial(per_device, sizes), mesh=grid, in_specs=in_specs, out_specs=out_specs,
        check_vma=False,
    )
```

```python
import functools
import math

import jax
import jax.numpy as jnp
import numpy as np
from jax import lax
from jax.experimental import pallas as pl
from jax.experimental.pallas import tpu as pltpu
from jax.sharding import Mesh
from jax.sharding import PartitionSpec as P

HEADS = 20
KV_HEADS = 5
GROUP = HEADS // KV_HEADS
HEAD_DIM = 64
TAGS = 4
Q_WIDTH = HEADS * HEAD_DIM
KV_WIDTH = KV_HEADS * HEAD_DIM
DOC_MOST = 1024
Z_CHIPS = 4
EPS = 1e-06
SCORE_SCALE = 0.125
LOG2E = math.log2(math.e)
MASKED = -1e30

bf16 = jnp.bfloat16
f32 = jnp.float32


def dot(left, right, left_dim, right_dim):
    return lax.dot_general(
        left, right, (((left_dim,), (right_dim,)), ((), ())), preferred_element_type=f32
    )


def matmul(left, right):
    return dot(left, right, 1, 0)


def block_slot(block, at_x, xs):
    return (block // xs) * xs + lax.rem(at_x - lax.rem(block, xs) + xs, xs)


def forward_kernel(xs, meta, start_ref, q_ref, k_ref, v_ref, o_ref, lse_ref, bias_ref, q_rows, acc):
    rows = q_ref.shape[1]
    size = k_ref.shape[2]
    low, high, q_start, at_x = meta[0], meta[1], meta[2], meta[3]

    @pl.when(pl.program_id(0) == 0)
    def _():
        q_pos = q_start + lax.broadcasted_iota(jnp.int32, (rows, size), 0)
        lanes = lax.broadcasted_iota(jnp.int32, (rows, size), 1)

        def fill(block, carry):
            key_pos = block * size + lanes
            allowed = (key_pos >= start_ref[...]) & (key_pos <= q_pos)
            bias_ref[block] = jnp.where(allowed, 0.0, MASKED)
            return carry

        lax.fori_loop(low, high, fill, 0)

    q_cols = q_ref[...].T
    for head in range(GROUP):
        q_rows[head] = q_cols[:, head * HEAD_DIM : (head + 1) * HEAD_DIM]
    sub = lax.broadcasted_iota(jnp.int32, (HEAD_DIM, size), 0)
    ones = jnp.where(sub == 0, 1.0, 0.0).astype(bf16)
    acc[...] = jnp.zeros_like(acc)

    def body(block, carry):
        slot = block_slot(block, at_x, xs)
        key_cols = k_ref[slot]
        value_rows = jnp.concatenate([v_ref[slot], ones], axis=0).T
        bias = bias_ref[block]
        for head in range(GROUP):
            raw = jnp.dot(q_rows[head], key_cols, preferred_element_type=f32)
            probs = jnp.exp2(raw * (SCORE_SCALE * LOG2E) + bias).astype(bf16)
            acc[head] += jnp.dot(probs, value_rows, preferred_element_type=f32)
        return carry

    lax.fori_loop(low, high, body, 0)
    for head in range(GROUP):
        turned = acc[head].T
        total = turned[HEAD_DIM : HEAD_DIM + 1, :]
        o_ref[head * HEAD_DIM : (head + 1) * HEAD_DIM, :] = (turned[:HEAD_DIM] / total).astype(bf16)
        lse_ref[0, head : head + 1, :] = jnp.log2(total)


def backward_kernel(
    xs, meta, start_ref, q_ref, k_ref, v_ref, go_ref, o_ref, lse_ref,
    dq_ref, dkv_ref, bias_ref, q_rows, go_rows, dq_acc, delta_ref,
):
    rows = q_ref.shape[1]
    size = k_ref.shape[2]
    low, high, q_start, at_x = meta[0], meta[1], meta[2], meta[3]

    @pl.when(pl.program_id(0) == 0)
    def _():
        q_pos = q_start + lax.broadcasted_iota(jnp.int32, (size, rows), 1)
        subs = lax.broadcasted_iota(jnp.int32, (size, rows), 0)

        def fill(block, carry):
            key_pos = block * size + subs
            allowed = (key_pos >= start_ref[...]) & (key_pos <= q_pos)
            bias_ref[block] = jnp.where(allowed, 0.0, MASKED)
            return carry

        lax.fori_loop(low, high, fill, 0)

    q_cols = q_ref[...].T
    go_cols = go_ref[...].T
    for head in range(GROUP):
        part = slice(head * HEAD_DIM, (head + 1) * HEAD_DIM)
        q_rows[head] = q_cols[:, part]
        go_rows[head] = go_cols[:, part]
        delta_ref[head : head + 1, :] = jnp.sum(
            go_ref[part, :].astype(f32) * o_ref[part, :].astype(f32), axis=0, keepdims=True
        )
    dkv_ref[...] = jnp.zeros_like(dkv_ref)
    dq_acc[...] = jnp.zeros_like(dq_acc)

    def body(block, carry):
        slot = block_slot(block, at_x, xs)
        key_cols = k_ref[slot]
        key_rows = key_cols.T
        value_rows = v_ref[slot].T
        bias = bias_ref[block]
        dk = jnp.zeros((size, HEAD_DIM), f32)
        dv = jnp.zeros((size, HEAD_DIM), f32)
        for head in range(GROUP):
            part = slice(head * HEAD_DIM, (head + 1) * HEAD_DIM)
            raw = jnp.dot(key_rows, q_ref[part, :], preferred_element_type=f32)
            probs = jnp.exp2(
                raw * (SCORE_SCALE * LOG2E) + (bias - lse_ref[0, head : head + 1, :])
            )
            grad_probs = jnp.dot(value_rows, go_ref[part, :], preferred_element_type=f32)
            grad_scores = (probs * (grad_probs - delta_ref[head : head + 1, :])).astype(bf16)
            dv += jnp.dot(probs.astype(bf16), go_rows[head], preferred_element_type=f32)
            dk += jnp.dot(grad_scores, q_rows[head], preferred_element_type=f32)
            dq_acc[part, :] += jnp.dot(key_cols, grad_scores, preferred_element_type=f32)
        dkv_ref[slot, 0] = (SCORE_SCALE * dk).T.astype(bf16)
        dkv_ref[slot, 1] = dv.T.astype(bf16)
        return carry

    lax.fori_loop(low, high, body, 0)
    dq_ref[...] = (SCORE_SCALE * dq_acc[...]).astype(bf16)


def attend_forward(xs, meta, start_col, q_t, batch, window):
    rows = start_col.shape[0]
    blocks, _, size = window.shape
    wide = GROUP * HEAD_DIM
    return pl.pallas_call(
        functools.partial(forward_kernel, xs),
        name="attend_forward",
        grid_spec=pltpu.PrefetchScalarGridSpec(
            num_scalar_prefetch=1,
            grid=(KV_HEADS,),
            in_specs=[
                pl.BlockSpec((rows, 1), lambda g, m: (0, 0)),
                pl.BlockSpec((wide, rows), lambda g, m: (g, batch)),
                pl.BlockSpec((blocks, HEAD_DIM, size), lambda g, m: (0, g, 0)),
                pl.BlockSpec((blocks, HEAD_DIM, size), lambda g, m: (0, KV_HEADS + g, 0)),
            ],
            out_specs=[
                pl.BlockSpec((wide, rows), lambda g, m: (g, 0)),
                pl.BlockSpec((1, GROUP, rows), lambda g, m: (g, 0, 0)),
            ],
            scratch_shapes=[
                pltpu.VMEM((blocks, rows, size), f32),
                pltpu.VMEM((GROUP, rows, HEAD_DIM), bf16),
                pltpu.VMEM((GROUP, rows, 2 * HEAD_DIM), f32),
            ],
        ),
        out_shape=[
            jax.ShapeDtypeStruct((Q_WIDTH, rows), bf16),
            jax.ShapeDtypeStruct((KV_HEADS, GROUP, rows), f32),
        ],
        cost_estimate=pl.CostEstimate(
            flops=4 * HEADS * rows * blocks * size * 128, bytes_accessed=4 * 1024 * 1024,
            transcendentals=HEADS * rows * blocks * size,
        ),
    )(meta, start_col, q_t, window, window)


def attend_backward(xs, meta, start_row, q_t, batch, window, go_t, o_t, lse):
    rows = start_row.shape[1]
    blocks, _, size = window.shape
    wide = GROUP * HEAD_DIM
    return pl.pallas_call(
        functools.partial(backward_kernel, xs),
        name="attend_backward",
        grid_spec=pltpu.PrefetchScalarGridSpec(
            num_scalar_prefetch=1,
            grid=(KV_HEADS,),
            in_specs=[
                pl.BlockSpec((1, rows), lambda g, m: (0, 0)),
                pl.BlockSpec((wide, rows), lambda g, m: (g, batch)),
                pl.BlockSpec((blocks, HEAD_DIM, size), lambda g, m: (0, g, 0)),
                pl.BlockSpec((blocks, HEAD_DIM, size), lambda g, m: (0, KV_HEADS + g, 0)),
                pl.BlockSpec((wide, rows), lambda g, m: (g, 0)),
                pl.BlockSpec((wide, rows), lambda g, m: (g, 0)),
                pl.BlockSpec((1, GROUP, rows), lambda g, m: (g, 0, 0)),
            ],
            out_specs=[
                pl.BlockSpec((wide, rows), lambda g, m: (g, 0)),
                pl.BlockSpec((blocks, 2, HEAD_DIM, size), lambda g, m: (0, 0, g, 0)),
            ],
            scratch_shapes=[
                pltpu.VMEM((blocks, size, rows), f32),
                pltpu.VMEM((GROUP, rows, HEAD_DIM), bf16),
                pltpu.VMEM((GROUP, rows, HEAD_DIM), bf16),
                pltpu.VMEM((wide, rows), f32),
                pltpu.VMEM((8, rows), f32),
            ],
        ),
        out_shape=[
            jax.ShapeDtypeStruct((Q_WIDTH, rows), bf16),
            jax.ShapeDtypeStruct((blocks, 2, KV_WIDTH, size), bf16),
        ],
        cost_estimate=pl.CostEstimate(
            flops=10 * HEADS * rows * blocks * size * 128, bytes_accessed=8 * 1024 * 1024,
            transcendentals=HEADS * rows * blocks * size,
        ),
    )(meta, start_row, q_t, window, window, go_t, o_t, lse)


LAYOUT = "yczx"
CTX = ("z", "x")
DOC_ROWS = 16


def after(value, *earlier):
    return lax.optimization_barrier((value, *earlier))[0]


class Transfers:
    def __init__(self, sizes):
        self.sizes = sizes

    def shift(self, value, axis, step):
        size = self.sizes[axis]
        return lax.ppermute(value, axis, [(i, (i + step) % size) for i in range(size)])

    def hop(self, value, axis, step):
        size = self.sizes[axis]
        pairs = [(i, i + step) for i in range(size) if 0 <= i + step < size]
        return lax.ppermute(value, axis, pairs)

    def place(self, pieces, axis, dim):
        size = self.sizes[axis]
        if size == 1:
            return jnp.expand_dims(pieces[0], dim)
        shape = pieces[0].shape
        rank = len(shape) + 1
        index = lax.broadcasted_iota(
            jnp.int32, tuple(size if d == dim else 1 for d in range(rank)), dim
        )
        back = jnp.mod(lax.axis_index(axis) - index, size)
        whole = jnp.broadcast_to(
            jnp.expand_dims(pieces[0], dim), shape[:dim] + (size,) + shape[dim:]
        )
        for k in range(1, size):
            whole = jnp.where(back == k, jnp.expand_dims(pieces[k], dim), whole)
        return whole

    def ring(self, value, axis):
        pieces = [value]
        for _ in range(1, self.sizes[axis]):
            pieces.append(self.shift(pieces[-1], axis, 1))
        return pieces

    def direct(self, value, axis):
        return [value] + [self.shift(value, axis, k) for k in range(1, self.sizes[axis])]

    def total(self, value, axis):
        size, step = self.sizes[axis], 1
        while step < size:
            value = value + lax.ppermute(value, axis, [(i, i ^ step) for i in range(size)])
            step *= 2
        return value

    def gather(self, value, axis, dim):
        return self.place(self.ring(value, axis), axis, dim)

    def take(self, value, axis, dim, step):
        size = self.sizes[axis]
        index = jnp.mod(lax.axis_index(axis) + step, size)
        return lax.dynamic_index_in_dim(value, index, dim, keepdims=False)

    def scatter(self, value, axis, dim):
        total = self.take(value, axis, dim, 0).astype(f32)
        for k in range(1, self.sizes[axis]):
            sent = self.take(value, axis, dim, k).astype(bf16)
            total = total + self.shift(sent, axis, k).astype(f32)
        return total

    def exchange(self, value, axis, dim, out_dim):
        pieces = [self.take(value, axis, dim, 0)]
        for k in range(1, self.sizes[axis]):
            pieces.append(self.shift(self.take(value, axis, dim, k), axis, k))
        return self.place(pieces, axis, out_dim)

    def spread(self, pieces, order):
        value = self.place(pieces, "z", 0)
        have = ["z"]
        for axis in order:
            dim = sum(1 for a in have if LAYOUT.index(a) < LAYOUT.index(axis))
            value = self.gather(value, axis, dim)
            have.append(axis)
        return value

    def scatter_chips(self, value, order):
        have = [axis for axis in LAYOUT if axis in order]
        for number, axis in enumerate(order):
            value = self.scatter(value, axis, have.index(axis))
            if number < len(order) - 1:
                value = value.astype(bf16)
            have.remove(axis)
        return value


def head_forward(lin, gain, cosine, sine):
    scale = lax.rsqrt(jnp.mean(lin * lin, axis=1, keepdims=True) + EPS)
    normal = lin * scale * gain[None, :, None]
    half = HEAD_DIM // 2
    first, second = normal[:, :half], normal[:, half:]
    turned = jnp.concatenate(
        [first * cosine - second * sine, second * cosine + first * sine], axis=1
    )
    return turned, scale


def head_backward(grad, lin, scale, gain, cosine, sine):
    half = HEAD_DIM // 2
    first, second = grad[:, :half], grad[:, half:]
    back = jnp.concatenate(
        [first * cosine + second * sine, second * cosine - first * sine], axis=1
    )
    gain_grad = jnp.sum(back * lin * scale, axis=(0, 2))
    scaled = back * gain[None, :, None]
    lin_grad = scale * scaled - lin * (scale**3) * jnp.mean(scaled * lin, axis=1, keepdims=True)
    return lin_grad, gain_grad


def row_scale(values):
    return lax.rsqrt(jnp.mean(values * values, axis=-1, keepdims=True) + EPS)


def norm_backward(grad, values, scale):
    return scale * grad - values * (scale**3) * jnp.mean(grad * values, axis=-1, keepdims=True)


def per_device(
    sizes, tokens, out_grad, doc_ids, corpus, corpus_weight, attn_gain, w_query, w_key, w_value,
    query_gain, key_gain, w_out, ffn_gain, w_gate, w_up, w_down,
):
    move = Transfers(sizes)
    ys, cs, zs, xs = (sizes[a] for a in LAYOUT)
    batches, local, width = tokens.shape
    both_rows = batches * local
    span = xs * local
    back_groups = -(-(DOC_MOST - 1) // span)
    at_z, at_x = lax.axis_index("z"), lax.axis_index("x")
    ffn_part = w_gate.shape[1] // (ys * cs)
    d_rows = w_gate.shape[0]
    parts = [slice(b * local, (b + 1) * local) for b in range(batches)]

    gain_a = attn_gain.astype(f32)[:, None]
    gain_f = ffn_gain.astype(f32)[:, None]
    w_kv = jnp.concatenate([w_key, w_value], axis=1)
    kv_near = move.direct((w_kv.astype(f32) * gain_a).astype(bf16), "z")
    w_q_low = (w_query.astype(f32) * gain_a).astype(bf16)
    q_near = move.direct(w_q_low, "z")
    kv_x = move.gather(move.place(kv_near, "z", 0), "x", 1)
    w_kv_all = move.gather(move.gather(kv_x, "y", 0), "c", 1).reshape(width, 2 * KV_WIDTH)

    w_gate_low = (w_gate.astype(f32) * gain_f).astype(bf16).reshape(d_rows, ys, cs, 1, ffn_part)
    w_up_low = (w_up.astype(f32) * gain_f).astype(bf16).reshape(d_rows, ys, cs, 1, ffn_part)
    both = jnp.concatenate([w_gate_low, w_up_low], axis=3).reshape(d_rows, ys, cs, 2 * ffn_part)
    both = move.exchange(after(both, kv_near[0]), "c", 2, 0)
    both = move.exchange(after(both, kv_x), "y", 2, 0)
    both = lax.all_gather(both, CTX, axis=0)
    w_down_all = lax.all_gather(w_down, CTX, axis=0, tiled=True)
    w_both = both.transpose(1, 2, 0, 3, 4).reshape(width, 2 * ffn_part)

    q_start = back_groups * span + at_x * local
    high = back_groups * xs + at_x + 1

    half_dim = HEAD_DIM // 2
    frequency = jnp.exp(
        jnp.arange(half_dim, dtype=f32) * (-2.0 * math.log(10000.0) / HEAD_DIM)
    )
    positions = (at_z * xs + at_x) * local + jnp.arange(local, dtype=jnp.int32)
    angles = frequency[:, None] * jnp.tile(positions, batches).astype(f32)[None, :]
    cosine, sine = jnp.cos(angles)[None], jnp.sin(angles)[None]
    gain_q, gain_k = query_gain.astype(f32), key_gain.astype(f32)

    tag_range = jnp.arange(TAGS, dtype=jnp.int32)
    grads_out = [
        jnp.sum(jnp.where(tag_range == corpus[b], corpus_weight, 0.0)) * out_grad[b].astype(f32)
        for b in range(batches)
    ]

    def core_blocks(chips):
        blocks = list(chips)
        for k in range(1, cs):
            blocks += [move.shift(chip, "c", k) for chip in chips]
        return blocks

    def core_sum(partial):
        blocks = partial.reshape(cs, ys, local, width)
        total = blocks[0].astype(f32)
        for k in range(1, cs):
            total = total + move.shift(blocks[k], "c", -k).astype(f32)
        return [total[0]] + [total[k].astype(bf16) for k in range(1, ys)]

    def chip_sum(rows):
        result = rows[0]
        for k in range(1, ys):
            result = result + move.shift(rows[k], "y", -k).astype(f32)
        return result

    inputs = after(tokens, *kv_near[1:]).reshape(both_rows, width).astype(f32)
    scale_in = row_scale(inputs)
    normed = (inputs * scale_in).astype(bf16)
    kv_lin = dot(w_kv_all, normed, 0, 1)
    key_lin = kv_lin[:KV_WIDTH].reshape(KV_HEADS, HEAD_DIM, both_rows)
    key_rot, key_scale = head_forward(key_lin, gain_k, cosine, sine)
    kv = jnp.concatenate(
        [
            key_rot.astype(bf16).reshape(KV_WIDTH, both_rows),
            kv_lin[KV_WIDTH:].astype(bf16),
            jnp.broadcast_to(doc_ids.reshape(1, both_rows).astype(bf16), (DOC_ROWS, both_rows)),
        ],
        axis=0,
    )
    hops = [kv]
    for _ in range(back_groups):
        hops.append(move.hop(hops[-1], "z", 1))
    w_q_all = move.spread(q_near, "xyc").reshape(width, Q_WIDTH)
    w_out_all = lax.all_gather(w_out, tuple(LAYOUT), axis=0, tiled=True)
    half = Q_WIDTH // 2
    query_lin = jnp.concatenate(
        [dot(w_q_all[:, :half], normed, 0, 1), dot(w_q_all[:, half:], normed, 0, 1)], axis=0
    ).reshape(HEADS, HEAD_DIM, both_rows)
    query_rot, query_scale = head_forward(query_lin, gain_q, cosine, sine)
    query_t = query_rot.astype(bf16).reshape(Q_WIDTH, both_rows)

    grad_chips = move.ring(
        after(jnp.concatenate(grads_out, axis=0).astype(bf16), hops[1]), "y"
    )

    blocks = []
    for group in hops[::-1]:
        blocks += move.direct(group, "x")
    windows = [jnp.stack([block[:, part] for block in blocks]) for part in parts]
    present = at_z + jnp.repeat(jnp.arange(back_groups + 1), xs) >= back_groups
    starts = []
    for b in range(batches):
        docs = jnp.where(present[:, None], windows[b][:, 2 * KV_WIDTH].astype(jnp.int32), -1)
        below = docs.reshape(1, -1) < doc_ids[b][:, None]
        starts.append(jnp.sum(below.astype(jnp.int32), axis=1))

    metas, mixed, lses, resids, scale_mids, normed2_all = [], [], [], [], [], []
    rows, normed2_chips = None, []
    for b, part in enumerate(parts):
        meta = jnp.stack([starts[b][0] // local, high, q_start, at_x]).astype(jnp.int32)
        if rows is not None:
            meta = after(meta, rows)
        mixed_t, lse = attend_forward(xs, meta, starts[b][:, None], query_t, b, windows[b])
        resid = inputs[part] + dot(mixed_t, w_out_all, 0, 0)
        scale_mid = row_scale(resid)
        rows = (resid * scale_mid).astype(bf16)
        normed2_chips.append(move.ring(rows, "y"))
        metas.append(meta)
        mixed.append(mixed_t)
        lses.append(lse)
        resids.append(resid)
        scale_mids.append(scale_mid)

    grad_blocks = core_blocks(grad_chips)
    grads_all = [jnp.concatenate([g[part] for g in grad_blocks], axis=0) for part in parts]

    hidden_grads = [dot(grads, w_down_all, 1, 1) for grads in grads_all]

    hiddens, gate_grads, up_grads, sums = [], [], [], []
    for b in range(batches):
        chips = normed2_chips[b]
        if b > 0:
            chips = chips[:1] + [after(chip, partial) for chip in chips[1:]]
        normed2_all.append(jnp.concatenate(core_blocks(chips), axis=0))
        wide = matmul(normed2_all[b], w_both)
        gate, up = wide[:, :ffn_part], wide[:, ffn_part:]
        sig = jax.nn.sigmoid(gate)
        silu = gate * sig
        hiddens.append((silu * up).astype(bf16))
        grad_hidden = hidden_grads[b]
        if b > 0:
            grad_hidden = after(grad_hidden, *sums[-1][1:])
        grad_gate = (grad_hidden * up * (sig * (1.0 + gate * (1.0 - sig)))).astype(bf16)
        grad_up = (grad_hidden * silu).astype(bf16)
        grad_wide = jnp.concatenate([grad_gate, grad_up], axis=1)
        partial = dot(grad_wide, w_both, 1, 1).astype(bf16)
        sums.append(core_sum(partial))
        gate_grads.append(grad_gate)
        up_grads.append(grad_up)

    grad_resids, low_grads = [], []
    for b in range(batches):
        grad_normed2 = chip_sum(sums[b])
        grad_resid = grads_out[b] + norm_backward(grad_normed2, resids[b], scale_mids[b])
        grad_resids.append(grad_resid)
        low_grads.append(grad_resid.astype(bf16))

    def token_sum(lefts, rights):
        total = dot(lefts[0], rights[0], 0, 0)
        for left, right in zip(lefts[1:], rights[1:]):
            total = total + dot(left, right, 0, 0)
        return total.astype(bf16)

    def scatter_columns(total):
        value = total.reshape(ys * cs, zs * xs * d_rows, ffn_part)
        return lax.psum_scatter(value, CTX, scatter_dimension=1, tiled=True)

    down_total = token_sum([after(hidden, partial) for hidden in hiddens], grads_all)
    grad_down = lax.psum_scatter(down_total, CTX, scatter_dimension=0, tiled=True).astype(f32)

    def split_cores(value, rows):
        value = value.astype(bf16).reshape(ys, cs, zs, xs, rows, -1)
        return move.scatter(value, "c", 1).astype(bf16)

    query_grads, carried = [], []
    for b in range(batches):
        low = after(low_grads[b], gate_total) if b > 0 else low_grads[b]
        grad_mixed_t = dot(w_out_all, low, 1, 1).astype(bf16)
        dq_t, dkv = attend_backward(
            xs, metas[b], starts[b][None, :], query_t, b, windows[b], grad_mixed_t, mixed[b],
            lses[b],
        )
        query_grads.append(dq_t)
        if b == 0:
            gate_total = token_sum(normed2_all, [after(gate_grads[0], dq_t)] + gate_grads[1:])
        groups = dkv.reshape(back_groups + 1, xs, 2 * KV_WIDTH, local)
        first = (move.hop(groups[0], "z", -1).astype(f32) + groups[1].astype(f32)).astype(bf16)
        carried.append([first] + [groups[k] for k in range(2, back_groups + 1)])

    held = query_grads[0]
    out_cores = split_cores(
        matmul(jnp.concatenate(mixed, axis=1), jnp.concatenate(low_grads, axis=0)), w_out.shape[0]
    )
    gate_sum = scatter_columns(gate_total)

    query_grad, gq_gain = head_backward(
        jnp.concatenate(query_grads, axis=1).astype(f32).reshape(HEADS, HEAD_DIM, both_rows),
        query_lin, query_scale, gain_q, cosine, sine,
    )
    query_grad = query_grad.astype(bf16).reshape(Q_WIDTH, both_rows)
    q_cores = split_cores(dot(normed, query_grad, 0, 1), d_rows)

    up_total = token_sum(normed2_all, [after(up_grads[0], held)] + up_grads[1:])
    up_sum = scatter_columns(up_total)

    out_chips = move.scatter(out_cores, "x", 2).astype(bf16)
    q_chips = move.scatter(q_cores, "y", 0).astype(bf16)
    out_rows = [
        core_sum(matmul(after(hidden, held), w_down_all).astype(bf16)) for hidden in hiddens
    ]
    kv_grads = []
    for b in range(batches):
        sent = carried[b][0]
        if b == batches - 1:
            sent = after(sent, out_cores, q_cores)
        for group in carried[b][1:]:
            sent = (move.hop(sent, "z", -1).astype(f32) + group.astype(f32)).astype(bf16)
        total = sent[0].astype(f32)
        for k in range(1, xs):
            total = total + move.shift(sent[k], "x", -k).astype(f32)
        kv_grads.append(total)
    outputs = [
        (resids[b] + chip_sum(out_rows[b])).astype(bf16) for b in range(batches)
    ]

    kv_sum = jnp.concatenate(kv_grads, axis=1)
    key_grad, gk_gain = head_backward(
        kv_sum[:KV_WIDTH].reshape(KV_HEADS, HEAD_DIM, both_rows), key_lin, key_scale, gain_k,
        cosine, sine,
    )
    kv_grad = jnp.concatenate(
        [key_grad.astype(bf16).reshape(KV_WIDTH, both_rows), kv_sum[KV_WIDTH:].astype(bf16)],
        axis=0,
    )
    kv_cores = split_cores(dot(normed, kv_grad, 0, 1), d_rows)
    grad_out_w = move.scatter_chips(after(out_chips, kv_cores), "yz")
    grad_q_w = move.scatter_chips(after(q_chips, kv_cores), "xz")
    grad_kv_w = move.scatter_chips(kv_cores, "yxz")
    grad_normed = dot(query_grad, w_q_all, 0, 1) + dot(kv_grad, w_kv_all, 0, 1)
    normed_back = norm_backward(grad_normed, inputs, scale_in)
    token_grads = [
        (grad_resids[b] + normed_back[part]).astype(bf16) for b, part in enumerate(parts)
    ]

    both_sum = jnp.concatenate([gate_sum, up_sum], axis=2).reshape(ys, cs, d_rows, -1)
    both_sum = move.exchange(after(both_sum, kv_cores), "y", 0, 2)
    both_sum = move.exchange(both_sum, "c", 0, 2).astype(f32)
    grad_gate_w = both_sum[..., :ffn_part].reshape(d_rows, -1)
    grad_up_w = both_sum[..., ffn_part:].reshape(d_rows, -1)

    attn_gain_grad = jnp.sum(grad_q_w * w_query.astype(f32), axis=1) + jnp.sum(
        grad_kv_w * w_kv.astype(f32), axis=1
    )
    ffn_gain_grad = jnp.sum(
        grad_gate_w * w_gate.astype(f32) + grad_up_w * w_up.astype(f32), axis=1
    )
    grad_kv_w = grad_kv_w * gain_a
    small = after(jnp.concatenate([gq_gain, gk_gain])[None, :], kv_cores)
    for axis in "xyzc":
        small = move.total(small, axis)

    return (
        jnp.stack(outputs),
        jnp.stack(token_grads),
        attn_gain_grad,
        grad_q_w * gain_a,
        grad_kv_w[:, :KV_WIDTH],
        grad_kv_w[:, KV_WIDTH:],
        small[0, :HEAD_DIM],
        small[0, HEAD_DIM:],
        grad_out_w,
        ffn_gain_grad,
        grad_gate_w * gain_f,
        grad_up_w * gain_f,
        grad_down,
    )


def solution(mesh):
    sizes = {"c": 2, "z": Z_CHIPS}
    sizes["y"] = mesh.shape["seq"] // sizes["c"]
    sizes["x"] = mesh.shape["ctx"] // sizes["z"]
    grid = Mesh(mesh.devices.reshape([sizes[a] for a in "yczx"]), ("y", "c", "z", "x"))
    seq, ctx, every = ("y", "c"), ("z", "x"), ("y", "c", "z", "x")
    acts, vector, matrix = P(seq, ctx, None), P(every), P(every, None)
    in_specs = (
        acts, acts, P(seq, ctx), P(seq), P(), vector, matrix, matrix, matrix, P(), P(), matrix,
        vector, matrix, matrix, matrix,
    )
    out_specs = (
        acts, acts, vector, matrix, matrix, matrix, P(), P(), matrix, vector, matrix, matrix,
        matrix,
    )
    return jax.shard_map(
        functools.partial(per_device, sizes), mesh=grid, in_specs=in_specs, out_specs=out_specs,
        check_vma=False,
    )
```
